32 devices in a mesh: row: 4 (over y, x), col: 8 (over z, core).
Axes of the slice: x: 2, y: 2, z: 4, core: 2. Of those that a mesh axis runs over, the one named last changes fastest.
Arguments:
- transmission: float32 [2, 2, 512, 1024], P(None, None, 'row', 'col'), may hold values from -6 to 6
- probe: float32 [2, 256, 256], replicated, may hold values from -6 to 6
- fresnel_phase: float32 [256, 256], replicated, may hold values from -3.140625 to 3.140625
- amplitudes: float32 [4, 8, 1, 256, 256], P('row', 'col'), may hold values from 0.3 to 4
- positions: int32 [4, 8, 1, 2], P('row', 'col'), may hold values from 0 to 72, as said below
- tv_weight: float32 [512, 1024], P('row', 'col'), may hold values from 0.3 to 3
Outputs:
- refined: float32 [2, 2, 512, 1024], P(None, None, 'row', 'col')
The draws below stay inside these ranges and needn't reach their ends.
Inputs may be any that keep to these rules, and one draw needn't show every extreme that they name: `positions`: over all tiles and views together, for each of the two coordinates, some view has offset 0 and some view has offset 2 * 36; a view covers rows and columns [offset, offset + 256) of its tile's region.
All inputs are finite; a program needn't handle non-finite values.
Results may differ from the reference program's by a relative error of at most 0.00016.
Values sent between devices are 32-bit elements; how exact they have to be, the bound alone decides.
A program may use at most 64 MiB of HBM per device.

```python
import math
import jax
import jax.numpy as jnp
from jax import lax

CORE = 128
PROBE = 256
SHIFT = 36
VIEWS = 1
SLICES = 2
TV_STEPS = 3
HALO = 100
EXTENT = 328
ROWS_ALL = 512
COLS_ALL = 1024
N_ROW = 4
N_COL = 8


def draw_positions(key, part):
    value_key, score_key = jax.random.split(key)
    entries = N_ROW * N_COL * VIEWS
    values = jax.random.randint(value_key, (entries, 2), 0, 2 * SHIFT + 1, dtype=jnp.int32)
    entry_index = jnp.arange(entries, dtype=jnp.int32)
    scores = jax.random.randint(score_key, (entries, 2), 0, 1 << 12, dtype=jnp.int32)
    scores = scores * entries + entry_index[:, None]
    ordering = jnp.argsort(scores, axis=0, stable=True)
    ranking = jnp.argsort(ordering, axis=0, stable=True)
    lowest = jnp.zeros_like(values)
    highest = jnp.full_like(values, 2 * SHIFT)
    chosen = jnp.where(ranking == 0, lowest, jnp.where(ranking == 1, highest, values))
    return chosen.reshape(N_ROW, N_COL, VIEWS, 2).astype(jnp.int32)


def levels(rng, dims, cuts, smallest, high):
    level = 1.0
    for position, shards_of in cuts:
        heights = jax.random.uniform(jax.random.fold_in(jax.random.fold_in(rng, 6), position), (shards_of,), jnp.float32, smallest / len(cuts), high / len(cuts))
        level = level * jnp.repeat(jnp.exp(heights), dims[position] // shards_of).reshape((-1,) + (1,) * (len(dims) - 1 - position))
    return level


def bell_draw(stream_key, shape, scale, limit, cuts=(), kind=jnp.bfloat16):
    gain = levels(stream_key, shape, cuts, -0.22, 0.18) if cuts else 1.0
    values = jax.random.normal(stream_key, shape, jnp.float32) * scale * gain
    return jnp.minimum(jnp.maximum(values, -limit), limit).astype(kind)


def setup_inputs(seed: int = 0) -> dict:
    keys = jax.random.split(jax.random.key(seed), 7)
    transmission = bell_draw(keys[0], (SLICES, 2, ROWS_ALL, COLS_ALL), 1.0, 6.0, ((2, 4), (3, 8)), jnp.float32)
    probe = bell_draw(keys[1], (2, PROBE, PROBE), 1.0, 6.0, (), jnp.float32)
    fresnel_phase = jnp.clip(jax.random.uniform(keys[2], (PROBE, PROBE), jnp.float32, -3.140625, 3.140625), -3.140625, 3.140625)
    amplitudes = jnp.clip(jnp.exp(math.log(4.0) - 2.5902671 * jax.random.uniform(keys[3], (N_ROW, N_COL, VIEWS, PROBE, PROBE), jnp.float32) ** levels(keys[3], (N_ROW, N_COL, VIEWS, PROBE, PROBE), ((0, 4), (1, 8)), -0.2, 0.2)), 0.3, 4.0)
    positions = draw_positions(jax.random.fold_in(keys[6], 71), 0)
    tv_weight = jnp.clip(jnp.exp(math.log(3.0) - 2.3025851 * jax.random.uniform(keys[5], (ROWS_ALL, COLS_ALL), jnp.float32) ** levels(keys[5], (ROWS_ALL, COLS_ALL), ((0, 4), (1, 8)), -0.2, 0.2)), 0.3, 3.0)
    return {"transmission": transmission, "probe": probe, "fresnel_phase": fresnel_phase, "amplitudes": amplitudes, "positions": positions, "tv_weight": tv_weight}


AMP_EPS = 0.1
LEARN_RATE = 0.2
TV_EPS = 1.0
TV_TAU = 0.1

def forward_two(field):
    return jnp.fft.fft2(field, norm='ortho')

def inverse_two(field):
    return jnp.fft.ifft2(field, norm='ortho')

def view_gradient(extended, probe_wave, kernel, measured, offset):
    anchor = jnp.zeros((), jnp.int32)
    windows = []
    for s in range(SLICES):
        window = lax.dynamic_slice(extended[s], (anchor, offset[0], offset[1]), (2, PROBE, PROBE))
        windows.append(window[0] + 1j * window[1])
    wave = probe_wave
    incoming = []
    for s in range(SLICES):
        incoming.append(wave)
        exit_wave = windows[s] * wave
        if s < SLICES - 1:
            wave = inverse_two(kernel * forward_two(exit_wave))
    far_field = forward_two(exit_wave)
    magnitude = jnp.sqrt(jnp.real(far_field) ** 2 + jnp.imag(far_field) ** 2 + AMP_EPS)
    adjoint = inverse_two(far_field * (1.0 - measured / magnitude))
    gradients = []
    for s in range(SLICES - 1, -1, -1):
        single = jnp.conj(incoming[s]) * adjoint
        gradients.insert(0, jnp.stack([jnp.real(single), jnp.imag(single)]))
        if s > 0:
            adjoint = inverse_two(jnp.conj(kernel) * forward_two(jnp.conj(windows[s]) * adjoint))
    return jnp.stack(gradients)

def tv_step(field, weight):
    padded = jnp.pad(field, ((0, 0), (0, 0), (0, 1), (0, 1)))
    down_diff = padded[:, :, 1:, :-1] - field
    right_diff = padded[:, :, :-1, 1:] - field
    spread = jnp.sqrt(lax.optimization_barrier(jnp.sum(down_diff * down_diff + right_diff * right_diff, axis=1, keepdims=True)) + TV_EPS)
    down_flux = weight * down_diff / spread
    right_flux = weight * right_diff / spread
    down_prev = jnp.pad(down_flux, ((0, 0), (0, 0), (1, 0), (0, 0)))[:, :, :-1, :]
    right_prev = jnp.pad(right_flux, ((0, 0), (0, 0), (0, 0), (1, 0)))[:, :, :, :-1]
    return field + TV_TAU * (down_flux - down_prev + right_flux - right_prev)

def reference(transmission, probe, fresnel_phase, amplitudes, positions, tv_weight):
    probe_wave = probe[0] + 1j * probe[1]
    kernel = jnp.cos(fresnel_phase) + 1j * jnp.sin(fresnel_phase)
    padded = jnp.pad(transmission, ((0, 0), (0, 0), (HALO, HALO), (HALO, HALO)))
    anchor = jnp.zeros((), jnp.int32)

    def add_tile(k, summed):
        tile_row = (k // N_COL).astype(jnp.int32)
        tile_col = (k % N_COL).astype(jnp.int32)
        corner = (anchor, anchor, tile_row * CORE, tile_col * CORE)
        extended = lax.dynamic_slice(padded, corner, (SLICES, 2, EXTENT, EXTENT))

        def add_view(v, local):
            view = jnp.asarray(v).astype(jnp.int32)
            offset = positions[tile_row, tile_col, view]
            gradient = view_gradient(extended, probe_wave, kernel, amplitudes[tile_row, tile_col, view], offset)
            place = (anchor, anchor, offset[0], offset[1])
            current = lax.dynamic_slice(local, place, (SLICES, 2, PROBE, PROBE))
            return lax.dynamic_update_slice(local, current + gradient, place)
        local = lax.fori_loop(0, VIEWS, add_view, jnp.zeros((SLICES, 2, EXTENT, EXTENT), jnp.float32))
        current = lax.dynamic_slice(summed, corner, (SLICES, 2, EXTENT, EXTENT))
        return lax.dynamic_update_slice(summed, current + local, corner)
    summed = lax.fori_loop(0, N_ROW * N_COL, add_tile, jnp.zeros(padded.shape, jnp.float32))
    gradient = summed[:, :, HALO:HALO + ROWS_ALL, HALO:HALO + COLS_ALL]
    field = transmission - LEARN_RATE * gradient
    for step in range(TV_STEPS):
        field = tv_step(field, tv_weight)
    return field
```

```python
import functools
import math

import jax
import jax.numpy as jnp
import numpy as np
from jax import lax
from jax.experimental import pallas as pl
from jax.experimental.pallas import tpu as pltpu
from jax.sharding import PartitionSpec as P

MESH = pl.DeviceIdType.MESH
F32, BF16 = jnp.float32, jnp.bfloat16
CORE = 128
PROBE = 256
HALF = 128
HALO = 100
NEAR = PROBE - CORE - HALO
STRIP = 104
REACH = 3
EDGE = 8
TVROWS = CORE + EDGE
FOLD = 16
AMP_EPS = 0.1
LEARN_RATE = 0.2
TV_EPS = 1.0
TV_TAU = 0.1
TV_STEPS = 3


def tables():
    k, j = np.arange(HALF)[:, None], np.arange(HALF)[None, :]
    parts = []
    for odd in (0, 1):
        angle = 2.0 * np.pi * (((2 * k + odd) * j) % PROBE) / PROBE
        c, s = np.cos(angle) / math.sqrt(PROBE), np.sin(angle) / math.sqrt(PROBE)
        full = np.block([[c, s], [-s, c]])
        parts.append(full)
    out = []
    for full in (parts[0], parts[0].T, parts[1], parts[1].T):
        full = full.astype(np.float32)
        high = full.astype(BF16)
        out += [high, (full - high.astype(np.float32)).astype(BF16)]
    order = np.zeros((PROBE, PROBE), np.float32)
    order[np.arange(HALF), 2 * np.arange(HALF)] = 1
    order[HALF + np.arange(HALF), 2 * np.arange(HALF) + 1] = 1
    out += [order.astype(BF16), order.T.astype(BF16)]
    return np.stack(out)


def split(x):
    high = x.astype(BF16)
    return high, (x - high.astype(F32)).astype(BF16)


def mm(a, b):
    return jnp.dot(a, b, preferred_element_type=F32)


def left(tab, i, x):
    wh, wl = tab[2 * i], tab[2 * i + 1]
    xh, xl = split(x)
    return mm(wh, xh) + (mm(wh, xl) + mm(wl, xh))


def right(tab, i, x):
    wh, wl = tab[2 * i], tab[2 * i + 1]
    xh, xl = split(x)
    return mm(xh, wh) + (mm(xl, wh) + mm(xh, wl))


def cat(a, b, axis):
    return jnp.concatenate([a, b], axis=axis)


def forward(tab, re, im):
    h = HALF
    e = left(tab, 0, cat(re[:h] + re[h:], im[:h] + im[h:], 0))
    o = left(tab, 2, cat(re[:h] - re[h:], im[:h] - im[h:], 0))
    re, im = cat(e[:h], o[:h], 0), cat(e[h:], o[h:], 0)
    e = right(tab, 1, cat(re[:, :h] + re[:, h:], im[:, :h] + im[:, h:], 1))
    o = right(tab, 3, cat(re[:, :h] - re[:, h:], im[:, :h] - im[:, h:], 1))
    return cat(e[:, :h], o[:, :h], 1), cat(e[:, h:], o[:, h:], 1)


def inverse(tab, re, im):
    h = HALF
    e = left(tab, 1, cat(re[:h], im[:h], 0))
    o = left(tab, 3, cat(re[h:], im[h:], 0))
    s, d = e + o, e - o
    re, im = cat(s[:h], d[:h], 0), cat(s[h:], d[h:], 0)
    e = right(tab, 0, cat(re[:, :h], im[:, :h], 1))
    o = right(tab, 2, cat(re[:, h:], im[:, h:], 1))
    s, d = e + o, e - o
    return cat(s[:, :h], d[:, :h], 1), cat(s[:, h:], d[:, h:], 1)


def reorder(tab, x):
    for axis in (0, 1):
        total = None
        rest = x
        for _ in range(3):
            part = rest.astype(BF16)
            rest = rest - part.astype(F32)
            term = mm(tab[8], part) if axis == 0 else mm(part, tab[9])
            total = term if total is None else total + term
        x = total
    return x


class Place:
    def __init__(self):
        self.r, self.c = lax.axis_index("row"), lax.axis_index("col")
        self.nr, self.nc = lax.axis_size("row"), lax.axis_size("col")
        self.odd = lax.rem(self.r, 2)
        step = 1 - 2 * self.odd
        rows = {"mate": self.r + step, "other": self.r - step, "ahead": self.r + 2 * step, "behind": self.r - 2 * step}
        self.to = {side: {"row": at} for side, at in rows.items()}
        self.has = {side: (at >= 0) & (at < self.nr) for side, at in rows.items()}
        for side, at in (("left", self.c - 1), ("right", self.c + 1)):
            self.to[side] = {"col": at}
            self.has[side] = (at >= 0) & (at < self.nc)

    def signal(self):
        sem = pltpu.get_barrier_semaphore()
        for side in OPPOSITE:
            @pl.when(self.has[side])
            def _():
                pl.semaphore_signal(sem, inc=1, device_id=self.to[side], device_id_type=MESH)

    def wait(self):
        sem = pltpu.get_barrier_semaphore()
        pl.semaphore_wait(sem, sum(self.has[side].astype(jnp.int32) for side in OPPOSITE))


OPPOSITE = {"left": "right", "right": "left", "mate": "mate", "other": "other", "ahead": "behind", "behind": "ahead"}


class Wire:
    def __init__(self, place, send, recv):
        self.place, self.send, self.recv = place, send, recv
        self.count, self.all = 0, []

    def __call__(self, side, src, dst):
        copy = Copy(self.place, side, src, dst, self.send.at[self.count], self.recv.at[self.count])
        self.count += 1
        self.all.append(copy)
        return copy


class Copy:
    def __init__(self, place, side, src, dst, send, recv):
        self.op = pltpu.make_async_remote_copy(
            src_ref=src, dst_ref=dst, send_sem=send, recv_sem=recv, device_id=place.to[side], device_id_type=MESH,
        )
        self.sends, self.gets = place.has[side], place.has[OPPOSITE[side]]

    def start(self):
        pl.when(self.sends)(lambda: self.op.start())

    def got(self):
        pl.when(self.gets)(lambda: self.op.wait_recv())

    def sent(self):
        pl.when(self.sends)(lambda: self.op.wait_send())


def iota(shape, axis):
    return lax.broadcasted_iota(jnp.int32, shape, axis)


def tall(tile):
    return cat_rows([tile] * (CORE // EDGE))


def cat_rows(parts):
    return jnp.concatenate(parts, axis=0)


def compact(x):
    parts = [x[FOLD * k : FOLD * k + FOLD] for k in range(CORE // FOLD)]
    return parts[0] + sum(pltpu.roll(part, FOLD * k, 1) for k, part in enumerate(parts) if k)


def expand(x):
    return cat_rows([x] + [pltpu.roll(x, CORE - FOLD * k, 1) for k in range(1, CORE // FOLD)])


def squeeze(x, n):
    lane = iota(x.shape, 1)
    x = jnp.where((lane < REACH) | (lane >= CORE - REACH), x, 0.0)
    return pltpu.roll(x, REACH + 8 * n, 1)


def whole_kernel(
    pos_any, tr_any, w_any, probe_any, phase_any, amp_any, tab_any, out,
    pos, tile, w, probe, phase_ref, amp, tab,
    hl, hr, cl, cr, mt, nm, outl, outr, place_me, place_l, place_r, xs,
    w_rows, w_mate, w_other, w_pack, w_left, w_right,
    g, gl, gr, il, ir, tot, edge, side_out, side_in, mate_out, mate_in,
    ptot, pedge, pmate, prim, pside_out, pside_in, pmate_out, pmate_in,
    send, recv, local,
):
    place = Place()
    has, odd = place.has, place.odd
    place.signal()
    loads = []
    pairs = (
        (tr_any, tile), (pos_any, pos), (phase_any, phase_ref), (tab_any, tab), (amp_any, amp), (probe_any, probe), (w_any, w),
    )
    for n, (src, dst) in enumerate(pairs):
        load = pltpu.make_async_copy(src, dst, local.at[n])
        load.start()
        loads.append(load)
    wire = Wire(place, send, recv)
    for side, refs in (
        ("left", (hl, cl, il, place_l, w_left)), ("right", (hr, cr, ir, place_r, w_right)),
        ("other", (nm, w_other)), ("ahead", (side_in, pside_in)),
    ):
        @pl.when(jnp.logical_not(has[side]))
        def _():
            for ref in refs:
                ref[...] = jnp.zeros(ref.shape, F32)
    loads[1].wait()
    p, q = pos[0], pos[1]
    place_me[...] = jnp.full((EDGE, CORE), p.astype(F32))
    loads[0].wait()
    place.wait()

    low_strip = pl.ds(pl.multiple_of((CORE - STRIP) * odd, EDGE), STRIP)
    high_strip = pl.ds(pl.multiple_of((CORE - STRIP) * (1 - odd), EDGE), STRIP)
    direct = {ch: wire("other", tile.at[ch, low_strip], nm.at[ch, low_strip]) for ch in DIRECT_A}
    to_mate = [wire("mate", tile.at[ch], mt.at[ch]) for ch in range(4)]
    to_left = [wire("left", tile.at[ch], hr.at[ch]) for ch in range(4)]
    to_right = [wire("right", tile.at[ch], hl.at[ch]) for ch in range(4)]
    relay = {ch: wire("ahead", mt.at[ch, high_strip], nm.at[ch, high_strip]) for ch in range(4) if ch not in direct}
    spots = [wire("left", place_me, place_r), wire("right", place_me, place_l)]
    corner_left = [wire("left", outl.at[ch], cr.at[ch]) for ch in range(4)]
    corner_right = [wire("right", outr.at[ch], cl.at[ch]) for ch in range(4)]
    w_steps = [wire("mate", w_rows, w_mate), wire("other", w_rows, w_other)]
    w_sides = [wire("left", w_pack, w_right), wire("right", w_pack, w_left)]
    for c in spots:
        c.start()
    for ch in range(4):
        if ch in direct:
            direct[ch].start()
        to_mate[ch].start()
        to_left[ch].start()
        to_right[ch].start()
    loads[6].wait()
    w_rows[0:EDGE] = w[0:EDGE]
    w_rows[EDGE:] = w[CORE - EDGE :]
    for c in w_steps:
        c.start()

    sign = (1 - 2 * odd).astype(F32)
    block = (CORE, CORE)
    row = iota(block, 0).astype(F32) - (NEAR - 0.5)
    lane = iota(block, 1)
    sub = iota((EDGE, CORE), 0)
    nearer = lane < NEAR + q
    own_rows = row < p.astype(F32)

    def is_even(shape):
        return jnp.full(shape, odd, jnp.int32) == 0

    def forward_rows(channels):
        for ch in channels:
            to_mate[ch].got()
            if ch in relay:
                relay[ch].start()

    def forward_corners(channels):
        if 0 in channels:
            for c in spots:
                c.got()
        to_l = sign * (row - tall(place_l[...])) < 0
        to_r = sign * (row - tall(place_r[...])) < 0
        for ch in channels:
            (direct[ch] if ch in direct else relay[ch]).got()
            m, n = mt[ch], nm[ch]
            outl[ch] = jnp.where(to_l, m, n)
            corner_left[ch].start()
            outr[ch] = jnp.where(to_r, m, n)
            corner_right[ch].start()

    mate_rows = sign * (row - p.astype(F32)) < 0

    def assemble(ch):
        to_left[ch].got()
        to_right[ch].got()
        h = jnp.where(nearer, hr[ch], hl[ch])
        v = jnp.where(mate_rows, mt[ch], nm[ch])
        corner_left[ch].got()
        corner_right[ch].got()
        c = jnp.where(nearer, cr[ch], cl[ch])
        xs[ch] = cat(cat(tile[ch], h, 1), cat(v, c, 1), 0)

    loads[2].wait()
    loads[3].wait()
    phase = reorder(tab, phase_ref[...])
    kr, ki = jnp.cos(phase), jnp.sin(phase)
    forward_rows((0, 1))
    loads[5].wait()
    turn_rows, turn_cols = p + (PROBE - HALO), q + (PROBE - HALO)
    pr, pi = (pltpu.roll(pltpu.roll(probe[n], turn_rows, 0), turn_cols, 1) for n in range(2))
    loads[4].wait()
    measured = reorder(tab, amp[...])
    forward_corners((0, 1))
    forward_rows((2, 3))
    assemble(0)
    assemble(1)
    ar, ai = xs[0], xs[1]
    fr, fi = forward(tab, ar * pr - ai * pi, ar * pi + ai * pr)
    forward_corners((2, 3))
    wr, wi = inverse(tab, kr * fr - ki * fi, kr * fi + ki * fr)
    assemble(2)
    assemble(3)
    br, bi = xs[2], xs[3]
    fr, fi = forward(tab, br * wr - bi * wi, br * wi + bi * wr)
    for c in w_steps:
        c.got()
    thin = is_even((EDGE, CORE))
    below = jnp.where(thin, w_mate[0:EDGE], w_other[0:EDGE])
    above = jnp.where(thin, w_other[EDGE:], w_mate[EDGE:])
    w_edge = jnp.where(sub < EDGE // 2, below, above)
    w_pack[0:FOLD] = compact(squeeze(w[...], 0))
    w_pack[FOLD:] = squeeze(w_edge, 0)
    for c in w_sides:
        c.start()
    factor = 1.0 - measured / jnp.sqrt(fr * fr + fi * fi + AMP_EPS)
    gr_, gi_ = inverse(tab, fr * factor, fi * factor)

    across = {}
    lanes = iota((PROBE, CORE), 1)
    near_lanes = lanes < NEAR + q

    def put(ch, grad):
        g[ch] = grad
        own, halo = grad[:, :CORE], grad[:, CORE:]
        across[ch] = (wire("right", gr.at[ch], il.at[ch]), wire("left", gl.at[ch], ir.at[ch]))
        gr[ch] = jnp.where(lanes >= CORE - REACH, own, jnp.where(near_lanes, halo, 0.0))
        across[ch][0].start()
        gl[ch] = jnp.where(lanes < REACH, own, jnp.where(near_lanes, 0.0, halo))
        across[ch][1].start()

    upward, onward = {}, {}

    lo, hi = CORE - STRIP, STRIP - EDGE

    def shares(t, down, up):
        even, thin = is_even(block), is_even((EDGE, CORE))
        rim = jnp.where(sub < REACH, down[:EDGE], jnp.where(sub >= EDGE - REACH, up[CORE - EDGE :], 0.0))
        first, last = t[:EDGE], t[CORE - EDGE :]
        up_far = cat_rows([up[:lo], jnp.where(sub < REACH, first, up[lo : lo + EDGE]), up[lo + EDGE :]])
        down_far = cat_rows([down[:hi], jnp.where(sub >= EDGE - REACH, last, down[hi : hi + EDGE]), down[hi + EDGE :]])
        mate_rim = jnp.where(thin, jnp.where(sub >= EDGE - REACH, last, 0.0), jnp.where(sub < REACH, first, 0.0))
        return rim, jnp.where(even, up_far, down_far), jnp.where(even, down, up), mate_rim

    def fold(s):
        in_l = row < tall(place_l[...])
        in_r = row < tall(place_r[...])
        low = lane < REACH
        in_side = jnp.where(low, row - tall(place_r[...]), row - tall(place_l[...])) < 0
        packed = [0.0, 0.0, 0.0]
        for n in range(2):
            ch = 2 * s + n
            for c in across[ch]:
                c.got()
            fl, fr = il[ch], ir[ch]
            own, halo = g[ch, :, :CORE], g[ch, :, CORE:]
            parts = (
                (own_rows, own), (in_l, jnp.where(lanes < CORE - REACH, fl, 0.0)), (in_r, jnp.where(lanes >= REACH, fr, 0.0)),
            )
            t = sum(x[:CORE] for _, x in parts)
            down = sum(jnp.where(m, x[CORE:], 0.0) for m, x in parts)
            up = sum(jnp.where(m, 0.0, x[CORE:]) for m, x in parts)
            tot[ch] = t
            edge[ch], side_out[ch], mate_out[ch, :CORE], mate_out[ch, CORE:] = shares(t, down, up)
            upward[ch] = wire("behind", side_out.at[ch, high_strip], side_in.at[ch, high_strip])
            upward[ch].start()
            h, o = halo[CORE:], jnp.where(low, fr[CORE:], fl[CORE:])
            pieces = (
                halo[:CORE] + jnp.where(low, fr[:CORE], fl[:CORE]),
                jnp.where(own_rows, h, 0.0) + jnp.where(in_side, o, 0.0),
                jnp.where(own_rows, 0.0, h) + jnp.where(in_side, 0.0, o),
            )
            packed = [a + squeeze(b, n) for a, b in zip(packed, pieces)]
        ptot[s] = packed[0]
        pedge[s], far, pmate[s], prim[s] = shares(*packed)
        pside_out[s] = compact(far)
        upward[4 + s] = wire("behind", pside_out.at[s], pside_in.at[s])
        upward[4 + s].start()

    def incoming(x):
        fill = jnp.where(is_even(block), jnp.where(row > 0, x, 0.0), jnp.where(row < HALO - NEAR, x, 0.0))
        rim = jnp.where(
            is_even((EDGE, CORE)),
            jnp.where(sub < REACH, x[lo : lo + EDGE], 0.0),
            jnp.where(sub >= EDGE - REACH, x[hi : hi + EDGE], 0.0),
        )
        return fill, rim

    def pass_on(s):
        for ch in (2 * s, 2 * s + 1):
            upward[ch].got()
            fill, rim = incoming(side_in[ch])
            mate_out[ch, :CORE] += fill
            mate_out[ch, CORE:] += rim
            onward[ch] = wire("mate", mate_out.at[ch], mate_in.at[ch])
            onward[ch].start()
        upward[4 + s].got()
        fill, rim = incoming(jnp.where(lane < FOLD, expand(pside_in[s]), 0.0))
        pmate_out[s, :FOLD] = compact(pmate[s] + fill)
        pmate_out[s, FOLD:] = prim[s] + rim
        onward[4 + s] = wire("mate", pmate_out.at[s], pmate_in.at[s])
        onward[4 + s].start()

    shape = (TVROWS, PROBE)

    def smooth(s):
        onward[4 + s].got()
        rest = cat_rows([ptot[s] + expand(pmate_in[s, :FOLD]), pedge[s] + pmate_in[s, FOLD:]])
        pair = []
        for n in range(2):
            ch = 2 * s + n
            onward[ch].got()
            grad = cat_rows([tot[ch] + mate_in[ch, :CORE], edge[ch] + mate_in[ch, CORE:]])
            grad = cat(grad, pltpu.roll(rest, CORE - REACH - 8 * n, 1), 1)
            wide = iota((EDGE, PROBE), 0) < EDGE // 2
            rim = jnp.where(wide, xs[ch, CORE : CORE + EDGE, :], xs[ch, PROBE - EDGE :, :])
            field = cat_rows([xs[ch, :CORE, :], rim])
            pair.append((field - LEARN_RATE * grad) * inside)
        for _ in range(TV_STEPS):
            down = [pltpu.roll(f, TVROWS - 1, 0) - f for f in pair]
            along_row = [pltpu.roll(f, PROBE - 1, 1) - f for f in pair]
            square = down[0] * down[0] + along_row[0] * along_row[0] + (down[1] * down[1] + along_row[1] * along_row[1])
            gain = weight / jnp.sqrt(square + TV_EPS)
            fresh = []
            for f, d, r in zip(pair, down, along_row):
                d, r = gain * d, gain * r
                update = d - pltpu.roll(d, 1, 0) + (r - pltpu.roll(r, 1, 1))
                fresh.append((f + TV_TAU * update) * inside)
            pair = fresh
        for n in range(2):
            out[2 * s + n] = pair[n][:CORE, :CORE]

    put(2, wr * gr_ + wi * gi_)
    put(3, wr * gi_ - wi * gr_)
    fr, fi = forward(tab, br * gr_ + bi * gi_, br * gi_ - bi * gr_)
    gr_, gi_ = inverse(tab, kr * fr + ki * fi, kr * fi - ki * fr)
    put(0, pr * gr_ + pi * gi_)
    put(1, pr * gi_ - pi * gr_)
    fold(1)
    for c in w_sides:
        c.got()
    row_at, col_at = iota(shape, 0), iota(shape, 1)
    row_at = place.r * CORE + jnp.where(row_at < CORE + EDGE // 2, row_at, row_at - TVROWS)
    col_at = place.c * CORE + jnp.where(col_at < CORE + HALF // 2, col_at, col_at - PROBE)
    inside = (row_at >= 0) & (row_at < place.nr * CORE) & (col_at >= 0) & (col_at < place.nc * CORE)
    inside = inside.astype(F32)
    margins = [cat_rows([expand(ref[:FOLD]), ref[FOLD:]]) for ref in (w_right, w_left)]
    margins = [pltpu.roll(m, CORE - REACH, 1) for m in margins]
    far = jnp.where(iota((TVROWS, CORE), 1) < HALF // 2, margins[0], margins[1])
    weight = cat(cat_rows([w[...], w_edge]), far, 1) * inside
    pass_on(1)
    fold(0)
    smooth(1)
    pass_on(0)
    smooth(0)
    for c in wire.all:
        c.sent()


DIRECT_A = ()


def body(transmission, probe, fresnel_phase, amplitudes, positions, tv_weight):
    vmem, anywhere = (pl.BlockSpec(memory_space=m) for m in (pltpu.VMEM, pl.ANY))
    tab = tables()

    def scratch(*shape):
        return pltpu.VMEM(shape, F32)

    four = lambda n: [scratch(4, CORE, CORE)] * n
    small = lambda n: [scratch(EDGE, CORE)] * n
    count = 48
    out = pl.pallas_call(
        whole_kernel,
        out_shape=jax.ShapeDtypeStruct((4, CORE, CORE), F32),
        in_specs=[anywhere] * 7,
        out_specs=vmem,
        scratch_shapes=[
            pltpu.SMEM((2,), jnp.int32), scratch(4, CORE, CORE), scratch(CORE, CORE), scratch(2, PROBE, PROBE),
            scratch(PROBE, PROBE), scratch(PROBE, PROBE), pltpu.VMEM(tab.shape, BF16),
            *four(8), *small(3), scratch(4, PROBE, PROBE),
            *[scratch(2 * EDGE, CORE)] * 3, *[scratch(FOLD + EDGE, CORE)] * 3,
            scratch(4, PROBE, PROBE), *[scratch(4, PROBE, CORE)] * 4,
            scratch(4, CORE, CORE), scratch(4, EDGE, CORE), *four(2), *[scratch(4, TVROWS, CORE)] * 2,
            scratch(2, CORE, CORE), scratch(2, EDGE, CORE), scratch(2, CORE, CORE), scratch(2, EDGE, CORE),
            *[scratch(2, FOLD, CORE)] * 2,
            *[scratch(2, FOLD + EDGE, CORE)] * 2,
            pltpu.SemaphoreType.DMA((count + 8,)),
            pltpu.SemaphoreType.DMA((count + 8,)),
            pltpu.SemaphoreType.DMA((7,)),
        ],
        compiler_params=pltpu.CompilerParams(collective_id=0, has_side_effects=True),
        name="ptycho",
    )(
        positions.reshape(2), transmission.reshape(4, CORE, CORE), tv_weight, probe, fresnel_phase,
        amplitudes.reshape(PROBE, PROBE), jnp.asarray(tab),
    )
    return out.reshape(2, 2, CORE, CORE)


def solution(mesh):
    placed = (
        P(None, None, "row", "col"),
        P(),
        P(),
        P("row", "col", None, None, None),
        P("row", "col", None, None),
        P("row", "col"),
    )
    return jax.shard_map(
        body, mesh=mesh, in_specs=placed, out_specs=P(None, None, "row", "col"), check_vma=False
    )
```

```python
import functools
import math

import jax
import jax.numpy as jnp
import numpy as np
from jax import lax
from jax.experimental import pallas as pl
from jax.experimental.pallas import tpu as pltpu
from jax.sharding import PartitionSpec as P

MESH = pl.DeviceIdType.MESH
F32, BF16 = jnp.float32, jnp.bfloat16
CORE = 128
PROBE = 256
HALF = 128
HALO = 100
NEAR = PROBE - CORE - HALO
STRIP = 104
REACH = 3
EDGE = 8
TVROWS = CORE + EDGE
FOLD = 16
AMP_EPS = 0.1
LEARN_RATE = 0.2
TV_EPS = 1.0
TV_TAU = 0.1
TV_STEPS = 3


def tables():
    k, j = np.arange(HALF)[:, None], np.arange(HALF)[None, :]
    parts = []
    for odd in (0, 1):
        angle = 2.0 * np.pi * (((2 * k + odd) * j) % PROBE) / PROBE
        c, s = np.cos(angle) / math.sqrt(PROBE), np.sin(angle) / math.sqrt(PROBE)
        full = np.block([[c, s], [-s, c]])
        parts.append(full)
    out = []
    for full in (parts[0], parts[0].T, parts[1], parts[1].T):
        full = full.astype(np.float32)
        high = full.astype(BF16)
        out += [high, (full - high.astype(np.float32)).astype(BF16)]
    order = np.zeros((PROBE, PROBE), np.float32)
    order[np.arange(HALF), 2 * np.arange(HALF)] = 1
    order[HALF + np.arange(HALF), 2 * np.arange(HALF) + 1] = 1
    out += [order.astype(BF16), order.T.astype(BF16)]
    return np.stack(out)


def split(x):
    high = x.astype(BF16)
    return high, (x - high.astype(F32)).astype(BF16)


def mm(a, b):
    return jnp.dot(a, b, preferred_element_type=F32)


def left(tab, i, x):
    wh, wl = tab[2 * i], tab[2 * i + 1]
    xh, xl = split(x)
    return mm(wh, xh) + (mm(wh, xl) + mm(wl, xh))


def right(tab, i, x):
    wh, wl = tab[2 * i], tab[2 * i + 1]
    xh, xl = split(x)
    return mm(xh, wh) + (mm(xl, wh) + mm(xh, wl))


def cat(a, b, axis):
    return jnp.concatenate([a, b], axis=axis)


def forward(tab, re, im):
    h = HALF
    e = left(tab, 0, cat(re[:h] + re[h:], im[:h] + im[h:], 0))
    o = left(tab, 2, cat(re[:h] - re[h:], im[:h] - im[h:], 0))
    re, im = cat(e[:h], o[:h], 0), cat(e[h:], o[h:], 0)
    e = right(tab, 1, cat(re[:, :h] + re[:, h:], im[:, :h] + im[:, h:], 1))
    o = right(tab, 3, cat(re[:, :h] - re[:, h:], im[:, :h] - im[:, h:], 1))
    return cat(e[:, :h], o[:, :h], 1), cat(e[:, h:], o[:, h:], 1)


def inverse(tab, re, im):
    h = HALF
    e = left(tab, 1, cat(re[:h], im[:h], 0))
    o = left(tab, 3, cat(re[h:], im[h:], 0))
    s, d = e + o, e - o
    re, im = cat(s[:h], d[:h], 0), cat(s[h:], d[h:], 0)
    e = right(tab, 0, cat(re[:, :h], im[:, :h], 1))
    o = right(tab, 2, cat(re[:, h:], im[:, h:], 1))
    s, d = e + o, e - o
    return cat(s[:, :h], d[:, :h], 1), cat(s[:, h:], d[:, h:], 1)


def reorder(tab, x):
    for axis in (0, 1):
        total = None
        rest = x
        for _ in range(3):
            part = rest.astype(BF16)
            rest = rest - part.astype(F32)
            term = mm(tab[8], part) if axis == 0 else mm(part, tab[9])
            total = term if total is None else total + term
        x = total
    return x


class Place:
    def __init__(self):
        self.r, self.c = lax.axis_index("row"), lax.axis_index("col")
        self.nr, self.nc = lax.axis_size("row"), lax.axis_size("col")
        self.odd = lax.rem(self.r, 2)
        step = 1 - 2 * self.odd
        rows = {"mate": self.r + step, "other": self.r - step, "ahead": self.r + 2 * step, "behind": self.r - 2 * step}
        self.to = {side: {"row": at} for side, at in rows.items()}
        self.has = {side: (at >= 0) & (at < self.nr) for side, at in rows.items()}
        for side, at in (("left", self.c - 1), ("right", self.c + 1)):
            self.to[side] = {"col": at}
            self.has[side] = (at >= 0) & (at < self.nc)

    def signal(self):
        sem = pltpu.get_barrier_semaphore()
        for side in OPPOSITE:
            @pl.when(self.has[side])
            def _():
                pl.semaphore_signal(sem, inc=1, device_id=self.to[side], device_id_type=MESH)

    def wait(self):
        sem = pltpu.get_barrier_semaphore()
        pl.semaphore_wait(sem, sum(self.has[side].astype(jnp.int32) for side in OPPOSITE))


OPPOSITE = {"left": "right", "right": "left", "mate": "mate", "other": "other", "ahead": "behind", "behind": "ahead"}


class Wire:
    def __init__(self, place, send, recv):
        self.place, self.send, self.recv = place, send, recv
        self.count, self.all = 0, []

    def __call__(self, side, src, dst):
        copy = Copy(self.place, side, src, dst, self.send.at[list(OPPOSITE).index(side)], self.recv.at[self.count])
        self.count += 1
        self.all.append(copy)
        return copy


class Copy:
    def __init__(self, place, side, src, dst, send, recv):
        self.op = pltpu.make_async_remote_copy(
            src_ref=src, dst_ref=dst, send_sem=send, recv_sem=recv, device_id=place.to[side], device_id_type=MESH,
        )
        self.sends, self.gets = place.has[side], place.has[OPPOSITE[side]]

    def start(self):
        pl.when(self.sends)(lambda: self.op.start())

    def got(self):
        pl.when(self.gets)(lambda: self.op.wait_recv())

    def sent(self):
        pl.when(self.sends)(lambda: self.op.wait_send())


def iota(shape, axis):
    return lax.broadcasted_iota(jnp.int32, shape, axis)


def tall(tile):
    return cat_rows([tile] * (CORE // EDGE))


def cat_rows(parts):
    return jnp.concatenate(parts, axis=0)


def compact(x):
    parts = [x[FOLD * k : FOLD * k + FOLD] for k in range(CORE // FOLD)]
    return parts[0] + sum(pltpu.roll(part, FOLD * k, 1) for k, part in enumerate(parts) if k)


def expand(x):
    return cat_rows([x] + [pltpu.roll(x, CORE - FOLD * k, 1) for k in range(1, CORE // FOLD)])


def squeeze(x, n):
    lane = iota(x.shape, 1)
    x = jnp.where((lane < REACH) | (lane >= CORE - REACH), x, 0.0)
    return pltpu.roll(x, REACH + 8 * n, 1)


def whole_kernel(
    pos_any, tr_any, w_any, probe_any, phase_any, amp_any, tab_any, out,
    pos, tile, w, probe, phase_ref, amp, tab,
    hl, hr, cl, cr, mt, nm, outl, outr, place_me, place_l, place_r, xs,
    w_rows, w_mate, w_other, w_pack, w_left, w_right,
    g, gl, gr, il, ir, tot, edge, side_out, side_in, near_out, near_in, mate_out, mate_in,
    ptot, pedge, pmate, prim, pside_out, pside_in, pmate_out, pmate_in,
    send, recv, local,
):
    place = Place()
    has, odd = place.has, place.odd
    place.signal()
    loads = []
    pairs = (
        (tr_any, tile), (pos_any, pos), (phase_any, phase_ref), (tab_any, tab), (amp_any, amp), (probe_any, probe), (w_any, w),
    )
    for n, (src, dst) in enumerate(pairs):
        load = pltpu.make_async_copy(src, dst, local.at[n])
        load.start()
        loads.append(load)
    wire = Wire(place, send, recv)
    for side, refs in (
        ("left", (hl, cl, il, place_l, w_left)), ("right", (hr, cr, ir, place_r, w_right)),
        ("other", (nm, w_other, *(side_in.at[ch] for ch in DIRECT_B))),
        ("ahead", (pside_in, *(side_in.at[ch] for ch in range(4) if ch not in DIRECT_B))),
    ):
        @pl.when(jnp.logical_not(has[side]))
        def _():
            for ref in refs:
                ref[...] = jnp.zeros(ref.shape, F32)
    loads[1].wait()
    p, q = pos[0], pos[1]
    place_me[...] = jnp.full((EDGE, CORE), p.astype(F32))
    loads[0].wait()
    place.wait()

    low_strip = pl.ds(pl.multiple_of((CORE - STRIP) * odd, EDGE), STRIP)
    high_strip = pl.ds(pl.multiple_of((CORE - STRIP) * (1 - odd), EDGE), STRIP)
    direct = {ch: wire("other", tile.at[ch, low_strip], nm.at[ch, low_strip]) for ch in DIRECT_A}
    to_mate = [wire("mate", tile.at[ch], mt.at[ch]) for ch in range(4)]
    slices = [pl.ds(2 * s, 2) for s in range(2)]
    to_left = [wire("left", tile.at[part], hr.at[part]) for part in slices]
    to_right = [wire("right", tile.at[part], hl.at[part]) for part in slices]
    relay = {ch: wire("ahead", mt.at[ch, high_strip], nm.at[ch, high_strip]) for ch in range(4) if ch not in direct}
    spots = [wire("left", place_me, place_r), wire("right", place_me, place_l)]
    corner_left = [wire("left", outl.at[ch], cr.at[ch]) for ch in range(4)]
    corner_right = [wire("right", outr.at[ch], cl.at[ch]) for ch in range(4)]
    w_steps = [wire("mate", w_rows, w_mate), wire("other", w_rows, w_other)]
    w_sides = [wire("left", w_pack, w_right), wire("right", w_pack, w_left)]
    for c in spots:
        c.start()
    for ch in range(4):
        if ch in direct:
            direct[ch].start()
        to_mate[ch].start()
        if ch % 2 == 0:
            to_left[ch // 2].start()
            to_right[ch // 2].start()
    loads[6].wait()
    w_rows[0:EDGE] = w[0:EDGE]
    w_rows[EDGE:] = w[CORE - EDGE :]
    for c in w_steps:
        c.start()

    sign = (1 - 2 * odd).astype(F32)
    block = (CORE, CORE)
    row = iota(block, 0).astype(F32) - (NEAR - 0.5)
    lane = iota(block, 1)
    sub = iota((EDGE, CORE), 0)
    nearer = lane < NEAR + q
    own_rows = row < p.astype(F32)

    def is_even(shape):
        return jnp.full(shape, odd, jnp.int32) == 0

    def forward_rows(channels):
        for ch in channels:
            to_mate[ch].got()
            if ch in relay:
                relay[ch].start()

    def forward_corners(channels):
        if 0 in channels:
            for c in spots:
                c.got()
        to_l = sign * (row - tall(place_l[...])) < 0
        to_r = sign * (row - tall(place_r[...])) < 0
        for ch in channels:
            (direct[ch] if ch in direct else relay[ch]).got()
            m, n = mt[ch], nm[ch]
            outl[ch] = jnp.where(to_l, m, n)
            corner_left[ch].start()
            outr[ch] = jnp.where(to_r, m, n)
            corner_right[ch].start()

    mate_rows = sign * (row - p.astype(F32)) < 0

    def assemble(ch):
        if ch % 2 == 0:
            to_left[ch // 2].got()
            to_right[ch // 2].got()
        h = jnp.where(nearer, hr[ch], hl[ch])
        v = jnp.where(mate_rows, mt[ch], nm[ch])
        corner_left[ch].got()
        corner_right[ch].got()
        c = jnp.where(nearer, cr[ch], cl[ch])
        xs[ch] = cat(cat(tile[ch], h, 1), cat(v, c, 1), 0)

    loads[2].wait()
    loads[3].wait()
    phase = reorder(tab, phase_ref[...])
    kr, ki = jnp.cos(phase), jnp.sin(phase)
    forward_rows((0,))
    forward_rows((1,))
    forward_corners((0,))
    loads[5].wait()
    turn_rows, turn_cols = p + (PROBE - HALO), q + (PROBE - HALO)
    pr, pi = (pltpu.roll(pltpu.roll(probe[n], turn_rows, 0), turn_cols, 1) for n in range(2))
    forward_corners((1,))
    forward_rows((2,))
    loads[4].wait()
    measured = reorder(tab, amp[...])
    forward_rows((3,))
    forward_corners((3,))
    forward_corners((2,))
    assemble(0)
    assemble(1)
    ar, ai = xs[0], xs[1]
    fr, fi = forward(tab, ar * pr - ai * pi, ar * pi + ai * pr)
    wr, wi = inverse(tab, kr * fr - ki * fi, kr * fi + ki * fr)
    assemble(2)
    assemble(3)
    br, bi = xs[2], xs[3]
    fr, fi = forward(tab, br * wr - bi * wi, br * wi + bi * wr)
    for c in w_steps:
        c.got()
    thin = is_even((EDGE, CORE))
    below = jnp.where(thin, w_mate[0:EDGE], w_other[0:EDGE])
    above = jnp.where(thin, w_other[EDGE:], w_mate[EDGE:])
    w_edge = jnp.where(sub < EDGE // 2, below, above)
    w_pack[0:FOLD] = compact(squeeze(w[...], 0))
    w_pack[FOLD:] = squeeze(w_edge, 0)
    for c in w_sides:
        c.start()
    factor = 1.0 - measured / jnp.sqrt(fr * fr + fi * fi + AMP_EPS)
    gr_, gi_ = inverse(tab, fr * factor, fi * factor)

    across = {}
    lanes = iota((PROBE, CORE), 1)
    near_lanes = lanes < NEAR + q
    body_rows, rim_rows = pl.ds(0, CORE - 2 * EDGE), pl.ds(CORE - 2 * EDGE, PROBE - CORE + 2 * EDGE)

    def put(ch, grad):
        g[ch] = grad
        own, halo = grad[:, :CORE], grad[:, CORE:]
        to_r = jnp.where(lanes >= CORE - REACH, own, jnp.where(near_lanes, halo, 0.0))
        to_l = jnp.where(lanes < REACH, own, jnp.where(near_lanes, 0.0, halo))
        for n, (ref, x) in enumerate(((gr, to_r), (gl, to_l))):
            ref[ch] = cat_rows([x[EDGE:], x[:EDGE]])
        across[ch] = cross(ch, rim_rows)

    def cross(which, rows):
        pair = wire("right", gr.at[which, rows], il.at[which, rows]), wire("left", gl.at[which, rows], ir.at[which, rows])
        for c in pair:
            c.start()
        return pair

    upward, onward = {}, {}

    lo, hi = CORE - STRIP, STRIP - EDGE

    def shares(first, last, down, up):
        even, thin = is_even(block), is_even((EDGE, CORE))
        rim = jnp.where(sub < REACH, down[:EDGE], jnp.where(sub >= EDGE - REACH, up[CORE - EDGE :], 0.0))
        up_far = cat_rows([up[:lo], jnp.where(sub < REACH, first, up[lo : lo + EDGE]), up[lo + EDGE :]])
        down_far = cat_rows([down[:hi], jnp.where(sub >= EDGE - REACH, last, down[hi : hi + EDGE]), down[hi + EDGE :]])
        far, near = jnp.where(even, up_far, down_far), jnp.where(even, down_far, up_far)
        mate_rim = jnp.where(thin, jnp.where(sub >= EDGE - REACH, last, 0.0), jnp.where(sub < REACH, first, 0.0))
        return rim, far, near, jnp.where(even, down, up), mate_rim

    bands = ((slice(0, EDGE), slice(PROBE - EDGE, PROBE)), (slice(CORE - EDGE, CORE), slice(CORE - 2 * EDGE, CORE - EDGE)))

    def joined(ch, mine, theirs):
        own, halo = g[ch, mine, :CORE], g[ch, mine, CORE:]
        fl, fr = il[ch, theirs], ir[ch, theirs]
        lane = iota(own.shape, 1)
        total = own + jnp.where(lane < CORE - REACH, fl, 0.0) + jnp.where(lane >= REACH, fr, 0.0)
        return total, halo + jnp.where(lane < REACH, fr, fl)

    packs = {}

    def fold(ch):
        s, n = divmod(ch, 2)
        for c in across[ch]:
            c.got()
        in_l = row < tall(place_l[...])
        in_r = row < tall(place_r[...])
        low = lane < REACH
        in_side = jnp.where(low, row - tall(place_r[...]), row - tall(place_l[...])) < 0
        far_rows = slice(CORE - EDGE, PROBE - EDGE)
        own, halo, fl, fr = g[ch, CORE:, :CORE], g[ch, CORE:, CORE:], il[ch, far_rows], ir[ch, far_rows]
        parts = ((own_rows, own), (in_l, jnp.where(lane < CORE - REACH, fl, 0.0)), (in_r, jnp.where(lane >= REACH, fr, 0.0)))
        down = sum(jnp.where(m, x, 0.0) for m, x in parts)
        up = sum(jnp.where(m, 0.0, x) for m, x in parts)
        ends = [joined(ch, *band) for band in bands]
        rim, far, near, base, mate_rim = shares(ends[0][0], ends[1][0], down, up)
        edge[ch], side_out[ch] = rim, far
        if ch in DIRECT_B:
            near_out[ch] = near
            upward[ch] = wire("other", side_out.at[ch, high_strip], side_in.at[ch, high_strip])
            onward[ch] = wire("mate", near_out.at[ch, low_strip], near_in.at[ch, low_strip])
            upward[ch].start()
            onward[ch].start()
        else:
            upward[ch] = wire("behind", side_out.at[ch, high_strip], side_in.at[ch, high_strip])
            upward[ch].start()
            mate_out[ch, :CORE], mate_out[ch, CORE:] = base, mate_rim
        o = jnp.where(low, fr, fl)
        pieces = [
            ends[0][1], ends[1][1],
            jnp.where(own_rows, halo, 0.0) + jnp.where(in_side, o, 0.0),
            jnp.where(own_rows, 0.0, halo) + jnp.where(in_side, 0.0, o),
        ]
        pieces = [squeeze(x, n) for x in pieces]
        if n == 0:
            packs[s] = pieces
            return
        pedge[s], far, _, pmate[s], prim[s] = shares(*[a + b for a, b in zip(packs[s], pieces)])
        pside_out[s] = compact(far)
        upward[4 + s] = wire("behind", pside_out.at[s], pside_in.at[s])
        upward[4 + s].start()

    def fill(s):
        for c in inner[s]:
            c.got()
        for n in range(2):
            ch = 2 * s + n
            parts = [joined(ch, *bands[0])]
            parts.append(joined(ch, slice(EDGE, CORE - EDGE), slice(0, CORE - 2 * EDGE)))
            parts.append(joined(ch, *bands[1]))
            tot[ch] = cat_rows([x for x, _ in parts])
            margin = squeeze(cat_rows([x for _, x in parts]), n)
            ptot[s] = margin if n == 0 else ptot[s] + margin

    def incoming(x, turned=False):
        even, thin = is_even(block), is_even((EDGE, CORE))
        from_up, from_low = jnp.where(row < HALO - NEAR, x, 0.0), jnp.where(row > 0, x, 0.0)
        rim_low, rim_up = jnp.where(sub < REACH, x[lo : lo + EDGE], 0.0), jnp.where(sub >= EDGE - REACH, x[hi : hi + EDGE], 0.0)
        if turned:
            return jnp.where(even, from_up, from_low), jnp.where(thin, rim_up, rim_low)
        return jnp.where(even, from_low, from_up), jnp.where(thin, rim_low, rim_up)

    def pass_on(ch):
        s, n = divmod(ch, 2)
        if ch not in DIRECT_B:
            upward[ch].got()
            more, rim = incoming(side_in[ch])
            mate_out[ch, :CORE] += more
            mate_out[ch, CORE:] += rim
            onward[ch] = wire("mate", mate_out.at[ch], mate_in.at[ch])
            onward[ch].start()
        if n == 0:
            return
        upward[4 + s].got()
        more, rim = incoming(jnp.where(lane < FOLD, expand(pside_in[s]), 0.0))
        pmate_out[s, :FOLD] = compact(pmate[s] + more)
        pmate_out[s, FOLD:] = prim[s] + rim
        onward[4 + s] = wire("mate", pmate_out.at[s], pmate_in.at[s])
        onward[4 + s].start()

    def total(ch):
        onward[ch].got()
        if ch not in DIRECT_B:
            return cat_rows([tot[ch] + mate_in[ch, :CORE], edge[ch] + mate_in[ch, CORE:]])
        upward[ch].got()
        (a, ra), (b, rb) = incoming(near_in[ch]), incoming(side_in[ch], True)
        return cat_rows([tot[ch] + a + b, edge[ch] + ra + rb])

    shape = (TVROWS, PROBE)

    def smooth(s):
        onward[4 + s].got()
        rest = cat_rows([ptot[s] + expand(pmate_in[s, :FOLD]), pedge[s] + pmate_in[s, FOLD:]])
        pair = []
        for n in range(2):
            ch = 2 * s + n
            grad = total(ch)
            grad = cat(grad, pltpu.roll(rest, CORE - REACH - 8 * n, 1), 1)
            wide = iota((EDGE, PROBE), 0) < EDGE // 2
            rim = jnp.where(wide, xs[ch, CORE : CORE + EDGE, :], xs[ch, PROBE - EDGE :, :])
            field = cat_rows([xs[ch, :CORE, :], rim])
            pair.append((field - LEARN_RATE * grad) * inside)
        for _ in range(TV_STEPS):
            down = [pltpu.roll(f, TVROWS - 1, 0) - f for f in pair]
            along_row = [pltpu.roll(f, PROBE - 1, 1) - f for f in pair]
            square = down[0] * down[0] + along_row[0] * along_row[0] + (down[1] * down[1] + along_row[1] * along_row[1])
            gain = weight / jnp.sqrt(square + TV_EPS)
            fresh = []
            for f, d, r in zip(pair, down, along_row):
                d, r = gain * d, gain * r
                update = d - pltpu.roll(d, 1, 0) + (r - pltpu.roll(r, 1, 1))
                fresh.append((f + TV_TAU * update) * inside)
            pair = fresh
        for n in range(2):
            out[2 * s + n] = pair[n][:CORE, :CORE]

    put(2, wr * gr_ + wi * gi_)
    put(3, wr * gi_ - wi * gr_)
    fr, fi = forward(tab, br * gr_ + bi * gi_, br * gi_ - bi * gr_)
    gr_, gi_ = inverse(tab, kr * fr + ki * fi, kr * fi - ki * fr)
    put(0, pr * gr_ + pi * gi_)
    put(1, pr * gi_ - pi * gr_)
    inner = {s: cross(pl.ds(2 * s, 2), body_rows) for s in (1, 0)}
    fold(2)
    fold(3)
    for c in w_sides:
        c.got()
    row_at, col_at = iota(shape, 0), iota(shape, 1)
    row_at = place.r * CORE + jnp.where(row_at < CORE + EDGE // 2, row_at, row_at - TVROWS)
    col_at = place.c * CORE + jnp.where(col_at < CORE + HALF // 2, col_at, col_at - PROBE)
    inside = (row_at >= 0) & (row_at < place.nr * CORE) & (col_at >= 0) & (col_at < place.nc * CORE)
    inside = inside.astype(F32)
    margins = [cat_rows([expand(ref[:FOLD]), ref[FOLD:]]) for ref in (w_right, w_left)]
    margins = [pltpu.roll(m, CORE - REACH, 1) for m in margins]
    far = jnp.where(iota((TVROWS, CORE), 1) < HALF // 2, margins[0], margins[1])
    weight = cat(cat_rows([w[...], w_edge]), far, 1) * inside
    fold(0)
    pass_on(2)
    pass_on(3)
    fold(1)
    pass_on(0)
    pass_on(1)
    fill(1)
    smooth(1)
    fill(0)
    smooth(0)
    assert wire.count == COPIES
    for c in wire.all:
        c.sent()


COPIES = 50
DIRECT_A = (3,)
DIRECT_B = (0, 2)


def body(transmission, probe, fresnel_phase, amplitudes, positions, tv_weight):
    vmem, anywhere = (pl.BlockSpec(memory_space=m) for m in (pltpu.VMEM, pl.ANY))
    tab = tables()

    def scratch(*shape):
        return pltpu.VMEM(shape, F32)

    four = lambda n: [scratch(4, CORE, CORE)] * n
    small = lambda n: [scratch(EDGE, CORE)] * n
    out = pl.pallas_call(
        whole_kernel,
        out_shape=pltpu.VMEM((4, CORE, CORE), F32),
        in_specs=[anywhere] * 7,
        out_specs=vmem,
        scratch_shapes=[
            pltpu.SMEM((2,), jnp.int32), scratch(4, CORE, CORE), scratch(CORE, CORE), scratch(2, PROBE, PROBE),
            scratch(PROBE, PROBE), scratch(PROBE, PROBE), pltpu.VMEM(tab.shape, BF16),
            *four(8), *small(3), scratch(4, PROBE, PROBE),
            *[scratch(2 * EDGE, CORE)] * 3, *[scratch(FOLD + EDGE, CORE)] * 3,
            scratch(4, PROBE, PROBE), *[scratch(4, PROBE, CORE)] * 4,
            scratch(4, CORE, CORE), scratch(4, EDGE, CORE), *four(4), *[scratch(4, TVROWS, CORE)] * 2,
            scratch(2, CORE, CORE), scratch(2, EDGE, CORE), scratch(2, CORE, CORE), scratch(2, EDGE, CORE),
            *[scratch(2, FOLD, CORE)] * 2,
            *[scratch(2, FOLD + EDGE, CORE)] * 2,
            pltpu.SemaphoreType.DMA((len(OPPOSITE),)),
            pltpu.SemaphoreType.DMA((COPIES,)),
            pltpu.SemaphoreType.DMA((7,)),
        ],
        compiler_params=pltpu.CompilerParams(collective_id=0, has_side_effects=True),
        name="ptycho",
    )(
        positions.reshape(2), transmission.reshape(4, CORE, CORE), tv_weight, probe, fresnel_phase,
        amplitudes.reshape(PROBE, PROBE), jnp.asarray(tab),
    )
    return out.reshape(2, 2, CORE, CORE)


def solution(mesh):
    placed = (
        P(None, None, "row", "col"),
        P(),
        P(),
        P("row", "col", None, None, None),
        P("row", "col", None, None),
        P("row", "col"),
    )
    return jax.shard_map(
        body, mesh=mesh, in_specs=placed, out_specs=P(None, None, "row", "col"), check_vma=False
    )
```

```python
import functools
import math

import jax
import jax.numpy as jnp
import numpy as np
from jax import lax
from jax.experimental import pallas as pl
from jax.experimental.pallas import tpu as pltpu
from jax.sharding import PartitionSpec as P

MESH = pl.DeviceIdType.MESH
F32, BF16 = jnp.float32, jnp.bfloat16
CORE = 128
PROBE = 256
HALF = 128
HALO = 100
NEAR = PROBE - CORE - HALO
STRIP = 104
REACH = 3
EDGE = 8
TVROWS = CORE + EDGE
FOLD = 16
AMP_EPS = 0.1
LEARN_RATE = 0.2
TV_EPS = 1.0
TV_TAU = 0.1
TV_STEPS = 3


def tables():
    k, j = np.arange(HALF)[:, None], np.arange(HALF)[None, :]
    parts = []
    for odd in (0, 1):
        angle = 2.0 * np.pi * (((2 * k + odd) * j) % PROBE) / PROBE
        c, s = np.cos(angle) / math.sqrt(PROBE), np.sin(angle) / math.sqrt(PROBE)
        full = np.block([[c, s], [-s, c]])
        parts.append(full)
    out = []
    for full in (parts[0], parts[0].T, parts[1], parts[1].T):
        full = full.astype(np.float32)
        high = full.astype(BF16)
        out += [high, (full - high.astype(np.float32)).astype(BF16)]
    order = np.zeros((PROBE, PROBE), np.float32)
    order[np.arange(HALF), 2 * np.arange(HALF)] = 1
    order[HALF + np.arange(HALF), 2 * np.arange(HALF) + 1] = 1
    out += [order.astype(BF16), order.T.astype(BF16)]
    return np.stack(out)


def split(x):
    high = x.astype(BF16)
    return high, (x - high.astype(F32)).astype(BF16)


def mm(a, b):
    return jnp.dot(a, b, preferred_element_type=F32)


def left(tab, i, x):
    wh, wl = tab[2 * i], tab[2 * i + 1]
    xh, xl = split(x)
    return mm(wh, xh) + (mm(wh, xl) + mm(wl, xh))


def right(tab, i, x):
    wh, wl = tab[2 * i], tab[2 * i + 1]
    xh, xl = split(x)
    return mm(xh, wh) + (mm(xl, wh) + mm(xh, wl))


def cat(a, b, axis):
    return jnp.concatenate([a, b], axis=axis)


def forward(tab, re, im):
    h = HALF
    e = left(tab, 0, cat(re[:h] + re[h:], im[:h] + im[h:], 0))
    o = left(tab, 2, cat(re[:h] - re[h:], im[:h] - im[h:], 0))
    re, im = cat(e[:h], o[:h], 0), cat(e[h:], o[h:], 0)
    e = right(tab, 1, cat(re[:, :h] + re[:, h:], im[:, :h] + im[:, h:], 1))
    o = right(tab, 3, cat(re[:, :h] - re[:, h:], im[:, :h] - im[:, h:], 1))
    return cat(e[:, :h], o[:, :h], 1), cat(e[:, h:], o[:, h:], 1)


def inverse(tab, re, im):
    h = HALF
    e = left(tab, 1, cat(re[:h], im[:h], 0))
    o = left(tab, 3, cat(re[h:], im[h:], 0))
    s, d = e + o, e - o
    re, im = cat(s[:h], d[:h], 0), cat(s[h:], d[h:], 0)
    e = right(tab, 0, cat(re[:, :h], im[:, :h], 1))
    o = right(tab, 2, cat(re[:, h:], im[:, h:], 1))
    s, d = e + o, e - o
    return cat(s[:, :h], d[:, :h], 1), cat(s[:, h:], d[:, h:], 1)


def reorder(tab, x):
    for axis in (0, 1):
        total = None
        rest = x
        for _ in range(3):
            part = rest.astype(BF16)
            rest = rest - part.astype(F32)
            term = mm(tab[8], part) if axis == 0 else mm(part, tab[9])
            total = term if total is None else total + term
        x = total
    return x


class Place:
    def __init__(self):
        self.r, self.c = lax.axis_index("row"), lax.axis_index("col")
        self.nr, self.nc = lax.axis_size("row"), lax.axis_size("col")
        self.odd = lax.rem(self.r, 2)
        step = 1 - 2 * self.odd
        rows = {"mate": self.r + step, "other": self.r - step, "ahead": self.r + 2 * step, "behind": self.r - 2 * step}
        self.to = {side: {"row": at} for side, at in rows.items()}
        self.has = {side: (at >= 0) & (at < self.nr) for side, at in rows.items()}
        for side, at in (("left", self.c - 1), ("right", self.c + 1)):
            self.to[side] = {"col": at}
            self.has[side] = (at >= 0) & (at < self.nc)

    def signal(self):
        sem = pltpu.get_barrier_semaphore()
        for side in OPPOSITE:
            @pl.when(self.has[side])
            def _():
                pl.semaphore_signal(sem, inc=1, device_id=self.to[side], device_id_type=MESH)

    def wait(self):
        sem = pltpu.get_barrier_semaphore()
        pl.semaphore_wait(sem, sum(self.has[side].astype(jnp.int32) for side in OPPOSITE))


OPPOSITE = {"left": "right", "right": "left", "mate": "mate", "other": "other", "ahead": "behind", "behind": "ahead"}


class Wire:
    def __init__(self, place, send, recv):
        self.place, self.send, self.recv = place, send, recv
        self.count, self.all = 0, []

    def __call__(self, side, src, dst, sends=True, gets=True):
        copy = Copy(self.place, side, src, dst, self.send.at[list(OPPOSITE).index(side)], self.recv.at[self.count])
        copy.sends, copy.gets = copy.sends & sends, copy.gets & gets
        self.count += 1
        self.all.append(copy)
        return copy


class Copy:
    def __init__(self, place, side, src, dst, send, recv):
        self.op = pltpu.make_async_remote_copy(
            src_ref=src, dst_ref=dst, send_sem=send, recv_sem=recv, device_id=place.to[side], device_id_type=MESH,
        )
        self.sends, self.gets = place.has[side], place.has[OPPOSITE[side]]

    def start(self):
        pl.when(self.sends)(lambda: self.op.start())

    def got(self):
        pl.when(self.gets)(lambda: self.op.wait_recv())

    def sent(self):
        pl.when(self.sends)(lambda: self.op.wait_send())


def iota(shape, axis):
    return lax.broadcasted_iota(jnp.int32, shape, axis)


def tall(tile):
    return cat_rows([tile] * (CORE // EDGE))


def cat_rows(parts):
    return jnp.concatenate(parts, axis=0)


def compact(x):
    parts = [x[FOLD * k : FOLD * k + FOLD] for k in range(CORE // FOLD)]
    return parts[0] + sum(pltpu.roll(part, FOLD * k, 1) for k, part in enumerate(parts) if k)


def expand(x):
    return cat_rows([x] + [pltpu.roll(x, CORE - FOLD * k, 1) for k in range(1, CORE // FOLD)])


def squeeze(x, n):
    lane = iota(x.shape, 1)
    x = jnp.where((lane < REACH) | (lane >= CORE - REACH), x, 0.0)
    return pltpu.roll(x, REACH + 8 * n, 1)


def whole_kernel(
    pos_any, tr_any, w_any, probe_any, phase_any, amp_any, tab_any, out,
    pos, tile, w, probe, phase_ref, amp, tab,
    hl, hr, cl, cr, mt, nm, bridge, outl, outr, place_me, place_l, place_r, xs,
    w_rows, w_mate, w_other, w_pack, w_left, w_right,
    g, gl, gr, il, ir, tot, edge, side_out, side_in, near_out, near_in, mate_out, mate_in,
    ptot, pedge, pside_out, pside_in, pnear_out, pnear_in,
    send, recv, local,
):
    place = Place()
    has, odd = place.has, place.odd
    place.signal()
    loads = []
    pairs = (
        (tr_any, tile), (pos_any, pos), (phase_any, phase_ref), (tab_any, tab), (amp_any, amp), (probe_any, probe), (w_any, w),
    )
    for n, (src, dst) in enumerate(pairs):
        load = pltpu.make_async_copy(src, dst, local.at[n])
        load.start()
        loads.append(load)
    wire = Wire(place, send, recv)
    for side, refs in (
        ("left", (hl, cl, il, place_l, w_left)), ("right", (hr, cr, ir, place_r, w_right)),
        ("other", (nm, w_other, pside_in, *(side_in.at[ch] for ch in DIRECT_B), *(mate_in.at[ch] for ch in range(4) if ch not in DIRECT_B))),
        ("ahead", tuple(side_in.at[ch] for ch in range(4) if ch not in DIRECT_B)),
    ):
        @pl.when(jnp.logical_not(has[side]))
        def _():
            for ref in refs:
                ref[...] = jnp.zeros(ref.shape, F32)

    @pl.when(has["other"])
    def _():
        for ch in range(4):
            if ch not in DIRECT_B:
                near_in[ch] = jnp.zeros((CORE, CORE), F32)

    loads[1].wait()
    p, q = pos[0], pos[1]
    place_me[...] = jnp.full((EDGE, CORE), p.astype(F32))
    loads[0].wait()
    place.wait()

    low_strip = pl.ds(pl.multiple_of((CORE - STRIP) * odd, EDGE), STRIP)
    high_strip = pl.ds(pl.multiple_of((CORE - STRIP) * (1 - odd), EDGE), STRIP)
    direct = {ch: wire("other", tile.at[ch, low_strip], nm.at[ch, low_strip]) for ch in DIRECT_A}
    to_mate = [
        wire("mate", *(ref.at[ch, high_strip if ch in (*direct, *VIA) else pl.ds(0, CORE)] for ref in (tile, mt))) for ch in range(4)
    ]
    slices = [pl.ds(2 * s, 2) for s in range(2)]
    to_left = [wire("left", tile.at[part], hr.at[part]) for part in slices]
    to_right = [wire("right", tile.at[part], hl.at[part]) for part in slices]
    via = {ch: wire("behind", tile.at[ch, low_strip], bridge.at[ch, low_strip]) for ch in VIA}
    across_via = {
        ch: wire("mate", bridge.at[ch, low_strip], nm.at[ch, low_strip], has["ahead"], has["other"]) for ch in VIA
    }
    relay = {
        ch: wire("ahead", mt.at[ch, high_strip], nm.at[ch, high_strip]) for ch in range(4) if ch not in (*direct, *via)
    }
    spots = [wire("left", place_me, place_r), wire("right", place_me, place_l)]
    corner_left = [wire("left", outl.at[ch], cr.at[ch]) for ch in range(4)]
    corner_right = [wire("right", outr.at[ch], cl.at[ch]) for ch in range(4)]
    w_steps = [wire("mate", w_rows, w_mate), wire("other", w_rows, w_other)]
    w_sides = [wire("left", w_pack, w_right), wire("right", w_pack, w_left)]
    for c in spots:
        c.start()
    for ch in ORDER:
        if ch in direct:
            direct[ch].start()
        if ch in via:
            via[ch].start()
        to_mate[ch].start()
        if ch % 2 == 0:
            to_left[ch // 2].start()
            to_right[ch // 2].start()
    loads[6].wait()
    w_rows[0:EDGE] = w[0:EDGE]
    w_rows[EDGE:] = w[CORE - EDGE :]
    for c in w_steps:
        c.start()

    sign = (1 - 2 * odd).astype(F32)
    block = (CORE, CORE)
    row = iota(block, 0).astype(F32) - (NEAR - 0.5)
    lane = iota(block, 1)
    sub = iota((EDGE, CORE), 0)
    nearer = lane < NEAR + q
    own_rows = row < p.astype(F32)

    def is_even(shape):
        return jnp.full(shape, odd, jnp.int32) == 0

    def forward_rows(channels):
        for ch in channels:
            to_mate[ch].got()
            if ch in relay:
                relay[ch].start()

    def forward_via(channels):
        for ch in channels:
            via[ch].got()
            across_via[ch].start()

    def forward_corners(channels):
        if 0 in channels:
            for c in spots:
                c.got()
        to_l = sign * (row - tall(place_l[...])) < 0
        to_r = sign * (row - tall(place_r[...])) < 0
        for ch in channels:
            {**direct, **across_via, **relay}[ch].got()
            m, n = mt[ch], nm[ch]
            outl[ch] = jnp.where(to_l, m, n)
            corner_left[ch].start()
            outr[ch] = jnp.where(to_r, m, n)
            corner_right[ch].start()

    mate_rows = sign * (row - p.astype(F32)) < 0

    def assemble(ch):
        if ch % 2 == 0:
            to_left[ch // 2].got()
            to_right[ch // 2].got()
        h = jnp.where(nearer, hr[ch], hl[ch])
        v = jnp.where(mate_rows, mt[ch], nm[ch])
        corner_left[ch].got()
        corner_right[ch].got()
        c = jnp.where(nearer, cr[ch], cl[ch])
        xs[ch] = cat(cat(tile[ch], h, 1), cat(v, c, 1), 0)

    loads[2].wait()
    loads[3].wait()
    phase = reorder(tab, phase_ref[...])
    kr, ki = jnp.cos(phase), jnp.sin(phase)
    forward_rows((0,))
    forward_via(VIA)
    forward_rows((2,))
    forward_corners((0,))
    loads[5].wait()
    turn_rows, turn_cols = p + (PROBE - HALO), q + (PROBE - HALO)
    pr, pi = (pltpu.roll(pltpu.roll(probe[n], turn_rows, 0), turn_cols, 1) for n in range(2))
    forward_rows((1,))
    forward_corners((1,))
    loads[4].wait()
    measured = reorder(tab, amp[...])
    forward_corners((2,))
    forward_rows((3,))
    forward_corners((3,))
    assemble(0)
    assemble(1)
    ar, ai = xs[0], xs[1]
    fr, fi = forward(tab, ar * pr - ai * pi, ar * pi + ai * pr)
    wr, wi = inverse(tab, kr * fr - ki * fi, kr * fi + ki * fr)
    assemble(2)
    assemble(3)
    br, bi = xs[2], xs[3]
    fr, fi = forward(tab, br * wr - bi * wi, br * wi + bi * wr)
    for c in w_steps:
        c.got()
    thin = is_even((EDGE, CORE))
    below = jnp.where(thin, w_mate[0:EDGE], w_other[0:EDGE])
    above = jnp.where(thin, w_other[EDGE:], w_mate[EDGE:])
    w_edge = jnp.where(sub < EDGE // 2, below, above)
    w_pack[0:FOLD] = compact(squeeze(w[...], 0))
    w_pack[FOLD:] = squeeze(w_edge, 0)
    for c in w_sides:
        c.start()
    factor = 1.0 - measured * lax.rsqrt(fr * fr + fi * fi + AMP_EPS)
    gr_, gi_ = inverse(tab, fr * factor, fi * factor)

    across = {}
    lanes = iota((PROBE, CORE), 1)
    near_lanes = lanes < NEAR + q
    body_rows, rim_rows = pl.ds(0, CORE - 2 * EDGE), pl.ds(CORE - 2 * EDGE, PROBE - CORE + 2 * EDGE)

    def put(ch, grad):
        g[ch] = grad
        own, halo = grad[:, :CORE], grad[:, CORE:]
        to_r = jnp.where(lanes >= CORE - REACH, own, jnp.where(near_lanes, halo, 0.0))
        to_l = jnp.where(lanes < REACH, own, jnp.where(near_lanes, 0.0, halo))
        for n, (ref, x) in enumerate(((gr, to_r), (gl, to_l))):
            ref[ch] = cat_rows([x[EDGE:], x[:EDGE]])
        across[ch] = cross(ch, rim_rows)

    def cross(which, rows):
        pair = wire("right", gr.at[which, rows], il.at[which, rows]), wire("left", gl.at[which, rows], ir.at[which, rows])
        for c in pair:
            c.start()
        return pair

    upward, onward, beside = {}, {}, {}

    lo, hi = CORE - STRIP, STRIP - EDGE

    def shares(first, last, down, up):
        even, thin = is_even(block), is_even((EDGE, CORE))
        rim = jnp.where(sub < REACH, down[:EDGE], jnp.where(sub >= EDGE - REACH, up[CORE - EDGE :], 0.0))
        up_far = cat_rows([up[:lo], jnp.where(sub < REACH, first, up[lo : lo + EDGE]), up[lo + EDGE :]])
        down_far = cat_rows([down[:hi], jnp.where(sub >= EDGE - REACH, last, down[hi : hi + EDGE]), down[hi + EDGE :]])
        far, near = jnp.where(even, up_far, down_far), jnp.where(even, down_far, up_far)
        mate_rim = jnp.where(thin, jnp.where(sub >= EDGE - REACH, last, 0.0), jnp.where(sub < REACH, first, 0.0))
        return rim, far, near, jnp.where(even, down, up), mate_rim

    bands = ((slice(0, EDGE), slice(PROBE - EDGE, PROBE)), (slice(CORE - EDGE, CORE), slice(CORE - 2 * EDGE, CORE - EDGE)))

    def joined(ch, mine, theirs):
        own, halo = g[ch, mine, :CORE], g[ch, mine, CORE:]
        fl, fr = il[ch, theirs], ir[ch, theirs]
        lane = iota(own.shape, 1)
        total = own + jnp.where(lane < CORE - REACH, fl, 0.0) + jnp.where(lane >= REACH, fr, 0.0)
        return total, halo + jnp.where(lane < REACH, fr, fl)

    packs = {}

    def fold(ch):
        s, n = divmod(ch, 2)
        for c in across[ch]:
            c.got()
        in_l = row < tall(place_l[...])
        in_r = row < tall(place_r[...])
        low = lane < REACH
        in_side = jnp.where(low, row - tall(place_r[...]), row - tall(place_l[...])) < 0
        far_rows = slice(CORE - EDGE, PROBE - EDGE)
        own, halo, fl, fr = g[ch, CORE:, :CORE], g[ch, CORE:, CORE:], il[ch, far_rows], ir[ch, far_rows]
        parts = ((own_rows, own), (in_l, jnp.where(lane < CORE - REACH, fl, 0.0)), (in_r, jnp.where(lane >= REACH, fr, 0.0)))
        down = sum(jnp.where(m, x, 0.0) for m, x in parts)
        up = sum(jnp.where(m, 0.0, x) for m, x in parts)
        ends = [joined(ch, *band) for band in bands]
        rim, far, near, base, mate_rim = shares(ends[0][0], ends[1][0], down, up)
        edge[ch], side_out[ch], near_out[ch] = rim, far, near
        strip = side_out.at[ch, high_strip], side_in.at[ch, high_strip]
        near_strip = near_out.at[ch, low_strip], near_in.at[ch, low_strip]
        if ch in DIRECT_B:
            upward[ch] = wire("other", *strip)
            beside[ch] = wire("mate", *near_strip)
        else:
            upward[ch] = wire("behind", *strip)
            beside[ch] = wire("mate", *near_strip, jnp.logical_not(has["ahead"]), jnp.logical_not(has["other"]))
            mate_out[ch, :CORE], mate_out[ch, CORE:] = base, mate_rim
        upward[ch].start()
        beside[ch].start()
        o = jnp.where(low, fr, fl)
        pieces = [
            ends[0][1], ends[1][1],
            jnp.where(own_rows, halo, 0.0) + jnp.where(in_side, o, 0.0),
            jnp.where(own_rows, 0.0, halo) + jnp.where(in_side, 0.0, o),
        ]
        pieces = [squeeze(x, n) for x in pieces]
        if n == 0:
            packs[s] = pieces
            return
        pedge[s], far, near, _, _ = shares(*[a + b for a, b in zip(packs[s], pieces)])
        pside_out[s], pnear_out[s] = compact(far), compact(near)
        upward[4 + s] = wire("other", pside_out.at[s], pside_in.at[s])
        beside[4 + s] = wire("mate", pnear_out.at[s], pnear_in.at[s])
        upward[4 + s].start()
        beside[4 + s].start()

    def fill(s):
        for c in inner[s]:
            c.got()
        for n in range(2):
            ch = 2 * s + n
            parts = [joined(ch, *bands[0])]
            parts.append(joined(ch, slice(EDGE, CORE - EDGE), slice(0, CORE - 2 * EDGE)))
            parts.append(joined(ch, *bands[1]))
            tot[ch] = cat_rows([x for x, _ in parts])
            margin = squeeze(cat_rows([x for _, x in parts]), n)
            ptot[s] = margin if n == 0 else ptot[s] + margin

    def incoming(x, turned=False):
        even, thin = is_even(block), is_even((EDGE, CORE))
        from_up, from_low = jnp.where(row < HALO - NEAR, x, 0.0), jnp.where(row > 0, x, 0.0)
        rim_low, rim_up = jnp.where(sub < REACH, x[lo : lo + EDGE], 0.0), jnp.where(sub >= EDGE - REACH, x[hi : hi + EDGE], 0.0)
        if turned:
            return jnp.where(even, from_up, from_low), jnp.where(thin, rim_up, rim_low)
        return jnp.where(even, from_low, from_up), jnp.where(thin, rim_low, rim_up)

    def pass_on(ch):
        upward[ch].got()
        more, rim = incoming(side_in[ch])
        mate_out[ch, :CORE] += more
        mate_out[ch, CORE:] += rim
        onward[ch] = wire("mate", mate_out.at[ch], mate_in.at[ch], has["ahead"], has["other"])
        onward[ch].start()

    def total(ch):
        beside[ch].got()
        a, ra = incoming(near_in[ch])
        if ch in DIRECT_B:
            upward[ch].got()
            b, rb = incoming(side_in[ch], True)
        else:
            onward[ch].got()
            b, rb = mate_in[ch, :CORE], mate_in[ch, CORE:]
        return cat_rows([tot[ch] + a + b, edge[ch] + ra + rb])

    shape = (TVROWS, PROBE)

    def smooth(s):
        upward[4 + s].got()
        beside[4 + s].got()
        (a, ra), (b, rb) = incoming(expand(pnear_in[s])), incoming(expand(pside_in[s]), True)
        rest = cat_rows([ptot[s] + a + b, pedge[s] + ra + rb])
        pair = []
        for n in range(2):
            ch = 2 * s + n
            grad = total(ch)
            grad = cat(grad, pltpu.roll(rest, CORE - REACH - 8 * n, 1), 1)
            wide = iota((EDGE, PROBE), 0) < EDGE // 2
            rim = jnp.where(wide, xs[ch, CORE : CORE + EDGE, :], xs[ch, PROBE - EDGE :, :])
            field = cat_rows([xs[ch, :CORE, :], rim])
            pair.append((field - LEARN_RATE * grad) * inside)
        for _ in range(TV_STEPS):
            down = [pltpu.roll(f, TVROWS - 1, 0) - f for f in pair]
            along_row = [pltpu.roll(f, PROBE - 1, 1) - f for f in pair]
            square = down[0] * down[0] + along_row[0] * along_row[0] + (down[1] * down[1] + along_row[1] * along_row[1])
            gain = weight * lax.rsqrt(square + TV_EPS)
            fresh = []
            for f, d, r in zip(pair, down, along_row):
                d, r = gain * d, gain * r
                update = d - pltpu.roll(d, 1, 0) + (r - pltpu.roll(r, 1, 1))
                fresh.append((f + TV_TAU * update) * inside)
            pair = fresh
        for n in range(2):
            out[2 * s + n] = pair[n][:CORE, :CORE]

    put(2, wr * gr_ + wi * gi_)
    put(3, wr * gi_ - wi * gr_)
    fr, fi = forward(tab, br * gr_ + bi * gi_, br * gi_ - bi * gr_)
    gr_, gi_ = inverse(tab, kr * fr + ki * fi, kr * fi - ki * fr)
    put(0, pr * gr_ + pi * gi_)
    put(1, pr * gi_ - pi * gr_)
    inner = {s: cross(pl.ds(2 * s, 2), body_rows) for s in (1, 0)}
    fold(2)
    fold(3)
    for c in w_sides:
        c.got()
    row_at, col_at = iota(shape, 0), iota(shape, 1)
    row_at = place.r * CORE + jnp.where(row_at < CORE + EDGE // 2, row_at, row_at - TVROWS)
    col_at = place.c * CORE + jnp.where(col_at < CORE + HALF // 2, col_at, col_at - PROBE)
    inside = (row_at >= 0) & (row_at < place.nr * CORE) & (col_at >= 0) & (col_at < place.nc * CORE)
    inside = inside.astype(F32)
    margins = [cat_rows([expand(ref[:FOLD]), ref[FOLD:]]) for ref in (w_right, w_left)]
    margins = [pltpu.roll(m, CORE - REACH, 1) for m in margins]
    far = jnp.where(iota((TVROWS, CORE), 1) < HALF // 2, margins[0], margins[1])
    weight = cat(cat_rows([w[...], w_edge]), far, 1) * inside
    fold(0)
    fold(1)
    pass_on(3)
    pass_on(0)
    fill(1)
    smooth(1)
    fill(0)
    smooth(0)
    assert wire.count == COPIES
    for c in wire.all:
        c.sent()


COPIES = 53
ORDER = (0, 2, 1, 3)
DIRECT_A = (3,)
VIA = (1,)
DIRECT_B = (1, 2)


def body(transmission, probe, fresnel_phase, amplitudes, positions, tv_weight):
    vmem, anywhere = (pl.BlockSpec(memory_space=m) for m in (pltpu.VMEM, pl.ANY))
    tab = tables()

    def scratch(*shape):
        return pltpu.VMEM(shape, F32)

    four = lambda n: [scratch(4, CORE, CORE)] * n
    small = lambda n: [scratch(EDGE, CORE)] * n
    out = pl.pallas_call(
        whole_kernel,
        out_shape=pltpu.VMEM((4, CORE, CORE), F32),
        in_specs=[anywhere] * 7,
        out_specs=vmem,
        scratch_shapes=[
            pltpu.SMEM((2,), jnp.int32), scratch(4, CORE, CORE), scratch(CORE, CORE), scratch(2, PROBE, PROBE),
            scratch(PROBE, PROBE), scratch(PROBE, PROBE), pltpu.VMEM(tab.shape, BF16),
            *four(9), *small(3), scratch(4, PROBE, PROBE),
            *[scratch(2 * EDGE, CORE)] * 3, *[scratch(FOLD + EDGE, CORE)] * 3,
            scratch(4, PROBE, PROBE), *[scratch(4, PROBE, CORE)] * 4,
            scratch(4, CORE, CORE), scratch(4, EDGE, CORE), *four(4), *[scratch(4, TVROWS, CORE)] * 2,
            scratch(2, CORE, CORE), scratch(2, EDGE, CORE), *[scratch(2, FOLD, CORE)] * 4,
            pltpu.SemaphoreType.DMA((len(OPPOSITE),)),
            pltpu.SemaphoreType.DMA((COPIES,)),
            pltpu.SemaphoreType.DMA((7,)),
        ],
        compiler_params=pltpu.CompilerParams(collective_id=0, has_side_effects=True),
        name="ptycho",
    )(
        positions.reshape(2), transmission.reshape(4, CORE, CORE), tv_weight, probe, fresnel_phase,
        amplitudes.reshape(PROBE, PROBE), jnp.asarray(tab),
    )
    return out.reshape(2, 2, CORE, CORE)


def solution(mesh):
    placed = (
        P(None, None, "row", "col"),
        P(),
        P(),
        P("row", "col", None, None, None),
        P("row", "col", None, None),
        P("row", "col"),
    )
    return jax.shard_map(
        body, mesh=mesh, in_specs=placed, out_specs=P(None, None, "row", "col"), check_vma=False
    )
```

```python
import functools
import math

import jax
import jax.numpy as jnp
import numpy as np
from jax import lax
from jax.experimental import pallas as pl
from jax.experimental.pallas import tpu as pltpu
from jax.sharding import PartitionSpec as P

MESH = pl.DeviceIdType.MESH
F32, BF16 = jnp.float32, jnp.bfloat16
CORE = 128
PROBE = 256
HALF = 128
HALO = 100
NEAR = PROBE - CORE - HALO
STRIP = 104
REACH = 3
EDGE = 8
TVROWS = CORE + EDGE
FOLD = 16
AMP_EPS = 0.1
LEARN_RATE = 0.2
TV_EPS = 1.0
TV_TAU = 0.1
TV_STEPS = 3


def tables():
    k, j = np.arange(HALF)[:, None], np.arange(HALF)[None, :]
    parts = []
    for odd in (0, 1):
        angle = 2.0 * np.pi * (((2 * k + odd) * j) % PROBE) / PROBE
        c, s = np.cos(angle) / math.sqrt(PROBE), np.sin(angle) / math.sqrt(PROBE)
        full = np.block([[c, s], [-s, c]])
        parts.append(full)
    out = []
    for full in (parts[0], parts[0].T, parts[1], parts[1].T):
        full = full.astype(np.float32)
        high = full.astype(BF16)
        out += [high, (full - high.astype(np.float32)).astype(BF16)]
    order = np.zeros((PROBE, PROBE), np.float32)
    order[np.arange(HALF), 2 * np.arange(HALF)] = 1
    order[HALF + np.arange(HALF), 2 * np.arange(HALF) + 1] = 1
    out += [order.astype(BF16), order.T.astype(BF16)]
    return np.stack(out)


def split(x):
    high = x.astype(BF16)
    return high, (x - high.astype(F32)).astype(BF16)


def mm(a, b):
    return jnp.dot(a, b, preferred_element_type=F32)


def left(tab, i, x):
    wh, wl = tab[2 * i], tab[2 * i + 1]
    xh, xl = split(x)
    return mm(wh, xh) + (mm(wh, xl) + mm(wl, xh))


def right(tab, i, x):
    wh, wl = tab[2 * i], tab[2 * i + 1]
    xh, xl = split(x)
    return mm(xh, wh) + (mm(xl, wh) + mm(xh, wl))


def cat(a, b, axis):
    return jnp.concatenate([a, b], axis=axis)


def forward(tab, re, im):
    h = HALF
    e = left(tab, 0, cat(re[:h] + re[h:], im[:h] + im[h:], 0))
    o = left(tab, 2, cat(re[:h] - re[h:], im[:h] - im[h:], 0))
    re, im = cat(e[:h], o[:h], 0), cat(e[h:], o[h:], 0)
    e = right(tab, 1, cat(re[:, :h] + re[:, h:], im[:, :h] + im[:, h:], 1))
    o = right(tab, 3, cat(re[:, :h] - re[:, h:], im[:, :h] - im[:, h:], 1))
    return cat(e[:, :h], o[:, :h], 1), cat(e[:, h:], o[:, h:], 1)


def inverse(tab, re, im):
    h = HALF
    e = left(tab, 1, cat(re[:h], im[:h], 0))
    o = left(tab, 3, cat(re[h:], im[h:], 0))
    s, d = e + o, e - o
    re, im = cat(s[:h], d[:h], 0), cat(s[h:], d[h:], 0)
    e = right(tab, 0, cat(re[:, :h], im[:, :h], 1))
    o = right(tab, 2, cat(re[:, h:], im[:, h:], 1))
    s, d = e + o, e - o
    return cat(s[:, :h], d[:, :h], 1), cat(s[:, h:], d[:, h:], 1)


def reorder(tab, x):
    for axis in (0, 1):
        total = None
        rest = x
        for _ in range(3):
            part = rest.astype(BF16)
            rest = rest - part.astype(F32)
            term = mm(tab[8], part) if axis == 0 else mm(part, tab[9])
            total = term if total is None else total + term
        x = total
    return x


class Place:
    def __init__(self):
        self.r, self.c = lax.axis_index("row"), lax.axis_index("col")
        self.nr, self.nc = lax.axis_size("row"), lax.axis_size("col")
        self.odd = lax.rem(self.r, 2)
        step = 1 - 2 * self.odd
        rows = {"mate": self.r + step, "other": self.r - step, "ahead": self.r + 2 * step, "behind": self.r - 2 * step}
        self.to = {side: {"row": at} for side, at in rows.items()}
        self.has = {side: (at >= 0) & (at < self.nr) for side, at in rows.items()}
        for side, at in (("left", self.c - 1), ("right", self.c + 1)):
            self.to[side] = {"col": at}
            self.has[side] = (at >= 0) & (at < self.nc)

    def signal(self):
        sem = pltpu.get_barrier_semaphore()
        for side in OPPOSITE:
            @pl.when(self.has[side])
            def _():
                pl.semaphore_signal(sem, inc=1, device_id=self.to[side], device_id_type=MESH)

    def wait(self):
        sem = pltpu.get_barrier_semaphore()
        pl.semaphore_wait(sem, sum(self.has[side].astype(jnp.int32) for side in OPPOSITE))


OPPOSITE = {"left": "right", "right": "left", "mate": "mate", "other": "other", "ahead": "behind", "behind": "ahead"}


class Wire:
    def __init__(self, place, send, recv):
        self.place, self.send, self.recv = place, send, recv
        self.count, self.all = 0, []

    def __call__(self, side, src, dst, sends=True, gets=True):
        copy = Copy(self.place, side, src, dst, self.send.at[list(OPPOSITE).index(side)], self.recv.at[self.count])
        copy.sends, copy.gets = copy.sends & sends, copy.gets & gets
        self.count += 1
        self.all.append(copy)
        return copy


class Copy:
    def __init__(self, place, side, src, dst, send, recv):
        self.op = pltpu.make_async_remote_copy(
            src_ref=src, dst_ref=dst, send_sem=send, recv_sem=recv, device_id=place.to[side], device_id_type=MESH,
        )
        self.sends, self.gets = place.has[side], place.has[OPPOSITE[side]]

    def start(self):
        pl.when(self.sends)(lambda: self.op.start())

    def got(self):
        pl.when(self.gets)(lambda: self.op.wait_recv())

    def sent(self):
        pl.when(self.sends)(lambda: self.op.wait_send())


def iota(shape, axis):
    return lax.broadcasted_iota(jnp.int32, shape, axis)


def tall(tile):
    return cat_rows([tile] * (CORE // EDGE))


def cat_rows(parts):
    return jnp.concatenate(parts, axis=0)


def compact(x):
    parts = [x[FOLD * k : FOLD * k + FOLD] for k in range(CORE // FOLD)]
    return parts[0] + sum(pltpu.roll(part, FOLD * k, 1) for k, part in enumerate(parts) if k)


def expand(x):
    return cat_rows([x] + [pltpu.roll(x, CORE - FOLD * k, 1) for k in range(1, CORE // FOLD)])


def squeeze(x, n):
    lane = iota(x.shape, 1)
    x = jnp.where((lane < REACH) | (lane >= CORE - REACH), x, 0.0)
    return pltpu.roll(x, REACH + 8 * n, 1)


def whole_kernel(
    pos_any, tr_any, w_any, probe_any, phase_any, amp_any, tab_any, out,
    pos, tile, w, probe, phase_ref, amp, tab,
    hl, hr, cl, cr, mt, nm, bridge, outl, outr, place_me, place_l, place_r, xs,
    w_rows, w_mate, w_other, w_pack, w_left, w_right,
    g, gl, gr, il, ir, tot, edge, side_out, side_in, near_out, near_in, mate_out, mate_in,
    ptot, pedge, pside_out, pside_in, pnear_out, pnear_in,
    send, recv, local,
):
    place = Place()
    has, odd = place.has, place.odd
    place.signal()
    loads = []
    pairs = (
        (tr_any, tile), (pos_any, pos), (phase_any, phase_ref), (tab_any, tab), (amp_any, amp), (probe_any, probe), (w_any, w),
    )
    for n, (src, dst) in enumerate(pairs):
        load = pltpu.make_async_copy(src, dst, local.at[n])
        load.start()
        loads.append(load)
    wire = Wire(place, send, recv)
    for side, refs in (
        ("left", (hl, cl, il, place_l, w_left)), ("right", (hr, cr, ir, place_r, w_right)),
        ("other", (nm, w_other, pside_in, *(side_in.at[ch] for ch in DIRECT_B), *(mate_in.at[ch] for ch in range(4) if ch not in DIRECT_B))),
        ("ahead", tuple(side_in.at[ch] for ch in range(4) if ch not in DIRECT_B)),
    ):
        @pl.when(jnp.logical_not(has[side]))
        def _():
            for ref in refs:
                ref[...] = jnp.zeros(ref.shape, F32)

    @pl.when(has["other"])
    def _():
        for ch in range(4):
            if ch not in DIRECT_B:
                near_in[ch] = jnp.zeros((CORE, CORE), F32)

    loads[1].wait()
    p, q = pos[0], pos[1]
    place_me[...] = jnp.full((EDGE, CORE), p.astype(F32))
    loads[0].wait()
    place.wait()

    low_strip = pl.ds(pl.multiple_of((CORE - STRIP) * odd, EDGE), STRIP)
    high_strip = pl.ds(pl.multiple_of((CORE - STRIP) * (1 - odd), EDGE), STRIP)
    direct = {ch: wire("other", tile.at[ch, low_strip], nm.at[ch, low_strip]) for ch in DIRECT_A}
    to_mate = [
        wire("mate", *(ref.at[ch, high_strip if ch in (*direct, *VIA) else pl.ds(0, CORE)] for ref in (tile, mt))) for ch in range(4)
    ]
    slices = [pl.ds(2 * s, 2) for s in range(2)]
    to_left = [wire("left", tile.at[part], hr.at[part]) for part in slices]
    to_right = [wire("right", tile.at[part], hl.at[part]) for part in slices]
    via = {ch: wire("behind", tile.at[ch, low_strip], bridge.at[ch, low_strip]) for ch in VIA}
    across_via = {
        ch: wire("mate", bridge.at[ch, low_strip], nm.at[ch, low_strip], has["ahead"], has["other"]) for ch in VIA
    }
    relay = {
        ch: wire("ahead", mt.at[ch, high_strip], nm.at[ch, high_strip]) for ch in range(4) if ch not in (*direct, *via)
    }
    spots = [wire("left", place_me, place_r), wire("right", place_me, place_l)]
    corner_left = [wire("left", outl.at[ch], cr.at[ch]) for ch in range(4)]
    corner_right = [wire("right", outr.at[ch], cl.at[ch]) for ch in range(4)]
    w_steps = [wire("mate", w_rows, w_mate), wire("other", w_rows, w_other)]
    w_sides = [wire("left", w_pack, w_right), wire("right", w_pack, w_left)]
    for c in spots:
        c.start()
    for ch in VIA:
        via[ch].start()
    for ch in ORDER:
        if ch in direct:
            direct[ch].start()
        to_mate[ch].start()
        if ch % 2 == 0:
            to_left[ch // 2].start()
            to_right[ch // 2].start()
    loads[6].wait()
    w_rows[0:EDGE] = w[0:EDGE]
    w_rows[EDGE:] = w[CORE - EDGE :]
    for c in w_steps:
        c.start()

    sign = (1 - 2 * odd).astype(F32)
    block = (CORE, CORE)
    row = iota(block, 0).astype(F32) - (NEAR - 0.5)
    lane = iota(block, 1)
    sub = iota((EDGE, CORE), 0)
    nearer = lane < NEAR + q
    own_rows = row < p.astype(F32)

    def is_even(shape):
        return jnp.full(shape, odd, jnp.int32) == 0

    def forward_rows(channels):
        for ch in channels:
            to_mate[ch].got()
            if ch in relay:
                relay[ch].start()

    def forward_via(channels):
        for ch in channels:
            via[ch].got()
            across_via[ch].start()

    def forward_corners(channels):
        if 0 in channels:
            for c in spots:
                c.got()
        to_l = sign * (row - tall(place_l[...])) < 0
        to_r = sign * (row - tall(place_r[...])) < 0
        for ch in channels:
            {**direct, **across_via, **relay}[ch].got()
            m, n = mt[ch], nm[ch]
            outl[ch] = jnp.where(to_l, m, n)
            corner_left[ch].start()
            outr[ch] = jnp.where(to_r, m, n)
            corner_right[ch].start()

    mate_rows = sign * (row - p.astype(F32)) < 0

    def assemble(ch):
        if ch % 2 == 0:
            to_left[ch // 2].got()
            to_right[ch // 2].got()
        h = jnp.where(nearer, hr[ch], hl[ch])
        v = jnp.where(mate_rows, mt[ch], nm[ch])
        corner_left[ch].got()
        corner_right[ch].got()
        c = jnp.where(nearer, cr[ch], cl[ch])
        xs[ch] = cat(cat(tile[ch], h, 1), cat(v, c, 1), 0)

    loads[2].wait()
    loads[3].wait()
    phase = reorder(tab, phase_ref[...])
    kr, ki = jnp.cos(phase), jnp.sin(phase)
    loads[5].wait()
    turn_rows, turn_cols = p + (PROBE - HALO), q + (PROBE - HALO)
    pr, pi = (pltpu.roll(pltpu.roll(probe[n], turn_rows, 0), turn_cols, 1) for n in range(2))
    forward_via(VIA)
    forward_rows((0,))
    forward_corners((0,))
    loads[4].wait()
    measured = reorder(tab, amp[...])
    for ch in (1, 2, 3):
        forward_rows((ch,))
        forward_corners((ch,))
    assemble(0)
    assemble(1)
    ar, ai = xs[0], xs[1]
    fr, fi = forward(tab, ar * pr - ai * pi, ar * pi + ai * pr)
    wr, wi = inverse(tab, kr * fr - ki * fi, kr * fi + ki * fr)
    assemble(2)
    assemble(3)
    br, bi = xs[2], xs[3]
    fr, fi = forward(tab, br * wr - bi * wi, br * wi + bi * wr)
    for c in w_steps:
        c.got()
    thin = is_even((EDGE, CORE))
    below = jnp.where(thin, w_mate[0:EDGE], w_other[0:EDGE])
    above = jnp.where(thin, w_other[EDGE:], w_mate[EDGE:])
    w_edge = jnp.where(sub < EDGE // 2, below, above)
    w_pack[0:FOLD] = compact(squeeze(w[...], 0))
    w_pack[FOLD:] = squeeze(w_edge, 0)
    for c in w_sides:
        c.start()
    factor = 1.0 - measured * lax.rsqrt(fr * fr + fi * fi + AMP_EPS)
    gr_, gi_ = inverse(tab, fr * factor, fi * factor)

    across = {}
    lanes = iota((PROBE, CORE), 1)
    near_lanes = lanes < NEAR + q
    body_rows, rim_rows = pl.ds(0, CORE - 2 * EDGE), pl.ds(CORE - 2 * EDGE, PROBE - CORE + 2 * EDGE)

    def put(ch, grad):
        g[ch] = grad
        own, halo = grad[:, :CORE], grad[:, CORE:]
        to_r = jnp.where(lanes >= CORE - REACH, own, jnp.where(near_lanes, halo, 0.0))
        to_l = jnp.where(lanes < REACH, own, jnp.where(near_lanes, 0.0, halo))
        for n, (ref, x) in enumerate(((gr, to_r), (gl, to_l))):
            ref[ch] = cat_rows([x[EDGE:], x[:EDGE]])
        across[ch] = cross(ch, rim_rows)

    def cross(which, rows):
        pair = wire("right", gr.at[which, rows], il.at[which, rows]), wire("left", gl.at[which, rows], ir.at[which, rows])
        for c in pair:
            c.start()
        return pair

    upward, onward, beside = {}, {}, {}

    lo, hi = CORE - STRIP, STRIP - EDGE

    def shares(first, last, down, up):
        even, thin = is_even(block), is_even((EDGE, CORE))
        rim = jnp.where(sub < REACH, down[:EDGE], jnp.where(sub >= EDGE - REACH, up[CORE - EDGE :], 0.0))
        up_far = cat_rows([up[:lo], jnp.where(sub < REACH, first, up[lo : lo + EDGE]), up[lo + EDGE :]])
        down_far = cat_rows([down[:hi], jnp.where(sub >= EDGE - REACH, last, down[hi : hi + EDGE]), down[hi + EDGE :]])
        far, near = jnp.where(even, up_far, down_far), jnp.where(even, down_far, up_far)
        mate_rim = jnp.where(thin, jnp.where(sub >= EDGE - REACH, last, 0.0), jnp.where(sub < REACH, first, 0.0))
        return rim, far, near, jnp.where(even, down, up), mate_rim

    bands = ((slice(0, EDGE), slice(PROBE - EDGE, PROBE)), (slice(CORE - EDGE, CORE), slice(CORE - 2 * EDGE, CORE - EDGE)))

    def joined(ch, mine, theirs):
        own, halo = g[ch, mine, :CORE], g[ch, mine, CORE:]
        fl, fr = il[ch, theirs], ir[ch, theirs]
        lane = iota(own.shape, 1)
        total = own + jnp.where(lane < CORE - REACH, fl, 0.0) + jnp.where(lane >= REACH, fr, 0.0)
        return total, halo + jnp.where(lane < REACH, fr, fl)

    packs = {}

    def fold(ch):
        s, n = divmod(ch, 2)
        for c in across[ch]:
            c.got()
        in_l = row < tall(place_l[...])
        in_r = row < tall(place_r[...])
        low = lane < REACH
        in_side = jnp.where(low, row - tall(place_r[...]), row - tall(place_l[...])) < 0
        far_rows = slice(CORE - EDGE, PROBE - EDGE)
        own, halo, fl, fr = g[ch, CORE:, :CORE], g[ch, CORE:, CORE:], il[ch, far_rows], ir[ch, far_rows]
        parts = ((own_rows, own), (in_l, jnp.where(lane < CORE - REACH, fl, 0.0)), (in_r, jnp.where(lane >= REACH, fr, 0.0)))
        down = sum(jnp.where(m, x, 0.0) for m, x in parts)
        up = sum(jnp.where(m, 0.0, x) for m, x in parts)
        ends = [joined(ch, *band) for band in bands]
        rim, far, near, base, mate_rim = shares(ends[0][0], ends[1][0], down, up)
        edge[ch], side_out[ch], near_out[ch] = rim, far, near
        strip = side_out.at[ch, high_strip], side_in.at[ch, high_strip]
        near_strip = near_out.at[ch, low_strip], near_in.at[ch, low_strip]
        if ch in DIRECT_B:
            upward[ch] = wire("other", *strip)
            beside[ch] = wire("mate", *near_strip)
        else:
            upward[ch] = wire("behind", *strip)
            beside[ch] = wire("mate", *near_strip, jnp.logical_not(has["ahead"]), jnp.logical_not(has["other"]))
            mate_out[ch, :CORE], mate_out[ch, CORE:] = base, mate_rim
        upward[ch].start()
        beside[ch].start()
        o = jnp.where(low, fr, fl)
        pieces = [
            ends[0][1], ends[1][1],
            jnp.where(own_rows, halo, 0.0) + jnp.where(in_side, o, 0.0),
            jnp.where(own_rows, 0.0, halo) + jnp.where(in_side, 0.0, o),
        ]
        pieces = [squeeze(x, n) for x in pieces]
        if n == 0:
            packs[s] = pieces
            return
        pedge[s], far, near, _, _ = shares(*[a + b for a, b in zip(packs[s], pieces)])
        pside_out[s], pnear_out[s] = compact(far), compact(near)
        upward[4 + s] = wire("other", pside_out.at[s], pside_in.at[s])
        beside[4 + s] = wire("mate", pnear_out.at[s], pnear_in.at[s])
        upward[4 + s].start()
        beside[4 + s].start()

    def fill(s):
        for c in inner[s]:
            c.got()
        for n in range(2):
            ch = 2 * s + n
            parts = [joined(ch, *bands[0])]
            parts.append(joined(ch, slice(EDGE, CORE - EDGE), slice(0, CORE - 2 * EDGE)))
            parts.append(joined(ch, *bands[1]))
            tot[ch] = cat_rows([x for x, _ in parts])
            margin = squeeze(cat_rows([x for _, x in parts]), n)
            ptot[s] = margin if n == 0 else ptot[s] + margin

    def incoming(x, turned=False):
        even, thin = is_even(block), is_even((EDGE, CORE))
        from_up, from_low = jnp.where(row < HALO - NEAR, x, 0.0), jnp.where(row > 0, x, 0.0)
        rim_low, rim_up = jnp.where(sub < REACH, x[lo : lo + EDGE], 0.0), jnp.where(sub >= EDGE - REACH, x[hi : hi + EDGE], 0.0)
        if turned:
            return jnp.where(even, from_up, from_low), jnp.where(thin, rim_up, rim_low)
        return jnp.where(even, from_low, from_up), jnp.where(thin, rim_low, rim_up)

    def pass_on(ch):
        upward[ch].got()
        more, rim = incoming(side_in[ch])
        mate_out[ch, :CORE] += more
        mate_out[ch, CORE:] += rim
        onward[ch] = wire("mate", mate_out.at[ch], mate_in.at[ch], has["ahead"], has["other"])
        onward[ch].start()

    def total(ch):
        beside[ch].got()
        a, ra = incoming(near_in[ch])
        if ch in DIRECT_B:
            upward[ch].got()
            b, rb = incoming(side_in[ch], True)
        else:
            onward[ch].got()
            b, rb = mate_in[ch, :CORE], mate_in[ch, CORE:]
        return cat_rows([tot[ch] + a + b, edge[ch] + ra + rb])

    shape = (TVROWS, PROBE)

    def smooth(s):
        upward[4 + s].got()
        beside[4 + s].got()
        (a, ra), (b, rb) = incoming(expand(pnear_in[s])), incoming(expand(pside_in[s]), True)
        rest = cat_rows([ptot[s] + a + b, pedge[s] + ra + rb])
        pair = []
        for n in range(2):
            ch = 2 * s + n
            grad = total(ch)
            grad = cat(grad, pltpu.roll(rest, CORE - REACH - 8 * n, 1), 1)
            wide = iota((EDGE, PROBE), 0) < EDGE // 2
            rim = jnp.where(wide, xs[ch, CORE : CORE + EDGE, :], xs[ch, PROBE - EDGE :, :])
            field = cat_rows([xs[ch, :CORE, :], rim])
            pair.append((field - LEARN_RATE * grad) * inside)
        for _ in range(TV_STEPS):
            down = [pltpu.roll(f, TVROWS - 1, 0) - f for f in pair]
            along_row = [pltpu.roll(f, PROBE - 1, 1) - f for f in pair]
            square = down[0] * down[0] + along_row[0] * along_row[0] + (down[1] * down[1] + along_row[1] * along_row[1])
            gain = weight * lax.rsqrt(square + TV_EPS)
            fresh = []
            for f, d, r in zip(pair, down, along_row):
                d, r = gain * d, gain * r
                update = d - pltpu.roll(d, 1, 0) + (r - pltpu.roll(r, 1, 1))
                fresh.append((f + TV_TAU * update) * inside)
            pair = fresh
        for n in range(2):
            out[2 * s + n] = pair[n][:CORE, :CORE]

    put(2, wr * gr_ + wi * gi_)
    put(3, wr * gi_ - wi * gr_)
    fr, fi = forward(tab, br * gr_ + bi * gi_, br * gi_ - bi * gr_)
    gr_, gi_ = inverse(tab, kr * fr + ki * fi, kr * fi - ki * fr)
    put(0, pr * gr_ + pi * gi_)
    put(1, pr * gi_ - pi * gr_)
    inner = {s: cross(pl.ds(2 * s, 2), body_rows) for s in (1, 0)}
    fold(2)
    fold(3)
    for c in w_sides:
        c.got()
    row_at, col_at = iota(shape, 0), iota(shape, 1)
    row_at = place.r * CORE + jnp.where(row_at < CORE + EDGE // 2, row_at, row_at - TVROWS)
    col_at = place.c * CORE + jnp.where(col_at < CORE + HALF // 2, col_at, col_at - PROBE)
    inside = (row_at >= 0) & (row_at < place.nr * CORE) & (col_at >= 0) & (col_at < place.nc * CORE)
    inside = inside.astype(F32)
    margins = [cat_rows([expand(ref[:FOLD]), ref[FOLD:]]) for ref in (w_right, w_left)]
    margins = [pltpu.roll(m, CORE - REACH, 1) for m in margins]
    far = jnp.where(iota((TVROWS, CORE), 1) < HALF // 2, margins[0], margins[1])
    weight = cat(cat_rows([w[...], w_edge]), far, 1) * inside
    fold(0)
    fold(1)
    pass_on(3)
    pass_on(0)
    fill(1)
    smooth(1)
    fill(0)
    smooth(0)
    assert wire.count == COPIES
    for c in wire.all:
        c.sent()


COPIES = 54
ORDER = (0, 1, 2, 3)
DIRECT_A = (0, 1)
VIA = (2, 3)
DIRECT_B = (1, 2)


def body(transmission, probe, fresnel_phase, amplitudes, positions, tv_weight):
    vmem, anywhere = (pl.BlockSpec(memory_space=m) for m in (pltpu.VMEM, pl.ANY))
    tab = tables()

    def scratch(*shape):
        return pltpu.VMEM(shape, F32)

    four = lambda n: [scratch(4, CORE, CORE)] * n
    small = lambda n: [scratch(EDGE, CORE)] * n
    out = pl.pallas_call(
        whole_kernel,
        out_shape=pltpu.VMEM((4, CORE, CORE), F32),
        in_specs=[anywhere] * 7,
        out_specs=vmem,
        scratch_shapes=[
            pltpu.SMEM((2,), jnp.int32), scratch(4, CORE, CORE), scratch(CORE, CORE), scratch(2, PROBE, PROBE),
            scratch(PROBE, PROBE), scratch(PROBE, PROBE), pltpu.VMEM(tab.shape, BF16),
            *four(9), *small(3), scratch(4, PROBE, PROBE),
            *[scratch(2 * EDGE, CORE)] * 3, *[scratch(FOLD + EDGE, CORE)] * 3,
            scratch(4, PROBE, PROBE), *[scratch(4, PROBE, CORE)] * 4,
            scratch(4, CORE, CORE), scratch(4, EDGE, CORE), *four(4), *[scratch(4, TVROWS, CORE)] * 2,
            scratch(2, CORE, CORE), scratch(2, EDGE, CORE), *[scratch(2, FOLD, CORE)] * 4,
            pltpu.SemaphoreType.DMA((len(OPPOSITE),)),
            pltpu.SemaphoreType.DMA((COPIES,)),
            pltpu.SemaphoreType.DMA((7,)),
        ],
        compiler_params=pltpu.CompilerParams(collective_id=0, has_side_effects=True),
        name="ptycho",
    )(
        positions.reshape(2), transmission.reshape(4, CORE, CORE), tv_weight, probe, fresnel_phase,
        amplitudes.reshape(PROBE, PROBE), jnp.asarray(tab),
    )
    return out.reshape(2, 2, CORE, CORE)


def solution(mesh):
    placed = (
        P(None, None, "row", "col"),
        P(),
        P(),
        P("row", "col", None, None, None),
        P("row", "col", None, None),
        P("row", "col"),
    )
    return jax.shard_map(
        body, mesh=mesh, in_specs=placed, out_specs=P(None, None, "row", "col"), check_vma=False
    )
```

```python
import functools
import math

import jax
import jax.numpy as jnp
import numpy as np
from jax import lax
from jax.experimental import pallas as pl
from jax.experimental.pallas import tpu as pltpu
from jax.sharding import PartitionSpec as P

MESH = pl.DeviceIdType.MESH
F32, BF16 = jnp.float32, jnp.bfloat16
CORE = 128
PROBE = 256
HALF = 128
HALO = 100
NEAR = PROBE - CORE - HALO
STRIP = 104
REACH = 3
EDGE = 8
TVROWS = CORE + EDGE
FOLD = 16
AMP_EPS = 0.1
LEARN_RATE = 0.2
TV_EPS = 1.0
TV_TAU = 0.1
TV_STEPS = 3


def tables():
    k, j = np.arange(HALF)[:, None], np.arange(HALF)[None, :]
    parts = []
    for odd in (0, 1):
        angle = 2.0 * np.pi * (((2 * k + odd) * j) % PROBE) / PROBE
        c, s = np.cos(angle) / math.sqrt(PROBE), np.sin(angle) / math.sqrt(PROBE)
        full = np.block([[c, s], [-s, c]])
        parts.append(full)
    out = []
    for full in (parts[0], parts[0].T, parts[1], parts[1].T):
        full = full.astype(np.float32)
        high = full.astype(BF16)
        out += [high, (full - high.astype(np.float32)).astype(BF16)]
    order = np.zeros((PROBE, PROBE), np.float32)
    order[np.arange(HALF), 2 * np.arange(HALF)] = 1
    order[HALF + np.arange(HALF), 2 * np.arange(HALF) + 1] = 1
    out += [order.astype(BF16), order.T.astype(BF16)]
    return np.stack(out)


def split(x):
    high = x.astype(BF16)
    return high, (x - high.astype(F32)).astype(BF16)


def mm(a, b):
    return jnp.dot(a, b, preferred_element_type=F32)


def left(tab, i, x):
    wh, wl = tab[2 * i], tab[2 * i + 1]
    xh, xl = split(x)
    return mm(wh, xh) + (mm(wh, xl) + mm(wl, xh))


def right(tab, i, x):
    wh, wl = tab[2 * i], tab[2 * i + 1]
    xh, xl = split(x)
    return mm(xh, wh) + (mm(xl, wh) + mm(xh, wl))


def cat(a, b, axis):
    return jnp.concatenate([a, b], axis=axis)


def forward(tab, re, im):
    h = HALF
    e = left(tab, 0, cat(re[:h] + re[h:], im[:h] + im[h:], 0))
    o = left(tab, 2, cat(re[:h] - re[h:], im[:h] - im[h:], 0))
    re, im = cat(e[:h], o[:h], 0), cat(e[h:], o[h:], 0)
    e = right(tab, 1, cat(re[:, :h] + re[:, h:], im[:, :h] + im[:, h:], 1))
    o = right(tab, 3, cat(re[:, :h] - re[:, h:], im[:, :h] - im[:, h:], 1))
    return cat(e[:, :h], o[:, :h], 1), cat(e[:, h:], o[:, h:], 1)


def inverse(tab, re, im):
    h = HALF
    e = left(tab, 1, cat(re[:h], im[:h], 0))
    o = left(tab, 3, cat(re[h:], im[h:], 0))
    s, d = e + o, e - o
    re, im = cat(s[:h], d[:h], 0), cat(s[h:], d[h:], 0)
    e = right(tab, 0, cat(re[:, :h], im[:, :h], 1))
    o = right(tab, 2, cat(re[:, h:], im[:, h:], 1))
    s, d = e + o, e - o
    return cat(s[:, :h], d[:, :h], 1), cat(s[:, h:], d[:, h:], 1)


def reorder(tab, x):
    for axis in (0, 1):
        total = None
        rest = x
        for _ in range(3):
            part = rest.astype(BF16)
            rest = rest - part.astype(F32)
            term = mm(tab[8], part) if axis == 0 else mm(part, tab[9])
            total = term if total is None else total + term
        x = total
    return x


class Place:
    def __init__(self):
        self.r, self.c = lax.axis_index("row"), lax.axis_index("col")
        self.nr, self.nc = lax.axis_size("row"), lax.axis_size("col")
        self.odd = lax.rem(self.r, 2)
        step = 1 - 2 * self.odd
        rows = {"mate": self.r + step, "other": self.r - step, "ahead": self.r + 2 * step, "behind": self.r - 2 * step}
        self.to = {side: {"row": at} for side, at in rows.items()}
        self.has = {side: (at >= 0) & (at < self.nr) for side, at in rows.items()}
        for side, at in (("left", self.c - 1), ("right", self.c + 1)):
            self.to[side] = {"col": at}
            self.has[side] = (at >= 0) & (at < self.nc)

    def signal(self):
        sem = pltpu.get_barrier_semaphore()
        for side in OPPOSITE:
            @pl.when(self.has[side])
            def _():
                pl.semaphore_signal(sem, inc=1, device_id=self.to[side], device_id_type=MESH)

    def wait(self):
        sem = pltpu.get_barrier_semaphore()
        pl.semaphore_wait(sem, sum(self.has[side].astype(jnp.int32) for side in OPPOSITE))


OPPOSITE = {"left": "right", "right": "left", "mate": "mate", "other": "other", "ahead": "behind", "behind": "ahead"}


class Wire:
    def __init__(self, place, send, recv):
        self.place, self.send, self.recv = place, send, recv
        self.count, self.all = 0, []

    def __call__(self, side, src, dst, sends=True, gets=True):
        copy = Copy(self.place, side, src, dst, self.send.at[list(OPPOSITE).index(side)], self.recv.at[self.count])
        copy.sends, copy.gets = copy.sends & sends, copy.gets & gets
        self.count += 1
        self.all.append(copy)
        return copy


class Copy:
    def __init__(self, place, side, src, dst, send, recv):
        self.op = pltpu.make_async_remote_copy(
            src_ref=src, dst_ref=dst, send_sem=send, recv_sem=recv, device_id=place.to[side], device_id_type=MESH,
        )
        self.sends, self.gets = place.has[side], place.has[OPPOSITE[side]]

    def start(self):
        pl.when(self.sends)(lambda: self.op.start())

    def got(self):
        pl.when(self.gets)(lambda: self.op.wait_recv())

    def sent(self):
        pl.when(self.sends)(lambda: self.op.wait_send())


def iota(shape, axis):
    return lax.broadcasted_iota(jnp.int32, shape, axis)


def tall(tile):
    return cat_rows([tile] * (CORE // EDGE))


def cat_rows(parts):
    return jnp.concatenate(parts, axis=0)


def compact(x):
    parts = [x[FOLD * k : FOLD * k + FOLD] for k in range(CORE // FOLD)]
    return parts[0] + sum(pltpu.roll(part, FOLD * k, 1) for k, part in enumerate(parts) if k)


def expand(x):
    return cat_rows([x] + [pltpu.roll(x, CORE - FOLD * k, 1) for k in range(1, CORE // FOLD)])


def squeeze(x, n):
    lane = iota(x.shape, 1)
    x = jnp.where((lane < REACH) | (lane >= CORE - REACH), x, 0.0)
    return pltpu.roll(x, REACH + 8 * n, 1)


def whole_kernel(
    pos_any, tr_any, w_any, probe_any, phase_any, amp_any, tab_any, out,
    pos, tile, w, probe, phase_ref, amp, tab,
    hl, hr, cl, cr, mt, nm, bridge, outl, outr, place_me, place_l, place_r, xs,
    w_rows, w_mate, w_other, w_pack, w_left, w_right,
    g, gl, gr, il, ir, tot, edge, side_out, side_in, near_out, near_in, mate_out, mate_in,
    fields, ptot, pedge, pbridge, pside_out, pside_in, pnear_out, pnear_in,
    send, recv, local,
):
    place = Place()
    has, odd = place.has, place.odd
    place.signal()
    loads = []
    pairs = (
        (tr_any, tile), (pos_any, pos), (phase_any, phase_ref), (tab_any, tab), (amp_any, amp), (probe_any, probe), (w_any, w),
    )
    for n, (src, dst) in enumerate(pairs):
        load = pltpu.make_async_copy(src, dst, local.at[n])
        load.start()
        loads.append(load)
    wire = Wire(place, send, recv)
    for side, refs in (
        ("left", (hl, cl, il, place_l, w_left)), ("right", (hr, cr, ir, place_r, w_right)),
        ("other", (nm, w_other, pside_in, *(side_in.at[ch] for ch in DIRECT_B), *(mate_in.at[ch] for ch in range(4) if ch not in DIRECT_B))),
        ("ahead", tuple(side_in.at[ch] for ch in range(4) if ch not in DIRECT_B)),
    ):
        @pl.when(jnp.logical_not(has[side]))
        def _():
            for ref in refs:
                ref[...] = jnp.zeros(ref.shape, F32)

    @pl.when(has["other"])
    def _():
        for ch in range(4):
            if ch not in DIRECT_B:
                near_in[ch] = jnp.zeros((CORE, CORE), F32)

    loads[1].wait()
    p, q = pos[0], pos[1]
    place_me[...] = jnp.full((EDGE, CORE), p.astype(F32))
    loads[0].wait()
    place.wait()

    low_strip = pl.ds(pl.multiple_of((CORE - STRIP) * odd, EDGE), STRIP)
    high_strip = pl.ds(pl.multiple_of((CORE - STRIP) * (1 - odd), EDGE), STRIP)
    half_strips = [
        pl.ds(pl.multiple_of((CORE - STRIP) * (1 - odd) + at, EDGE), size) for at, size in ((0, CUT), (CUT, STRIP - CUT))
    ]
    direct = {ch: wire("other", tile.at[ch, low_strip], nm.at[ch, low_strip]) for ch in DIRECT_A}
    to_mate = [
        wire("mate", *(ref.at[ch, high_strip if ch in (*direct, *VIA) else pl.ds(0, CORE)] for ref in (tile, mt))) for ch in range(4)
    ]
    slices = [pl.ds(2 * s, 2) for s in range(2)]
    to_left = [wire("left", tile.at[part], hr.at[part]) for part in slices]
    to_right = [wire("right", tile.at[part], hl.at[part]) for part in slices]
    via = {ch: wire("behind", tile.at[ch, low_strip], bridge.at[ch, low_strip]) for ch in VIA}
    across_via = {
        ch: wire("mate", bridge.at[ch, low_strip], nm.at[ch, low_strip], has["ahead"], has["other"]) for ch in VIA
    }
    relay = {
        ch: wire("ahead", mt.at[ch, high_strip], nm.at[ch, high_strip]) for ch in range(4) if ch not in (*direct, *via)
    }
    spots = [wire("left", place_me, place_r), wire("right", place_me, place_l)]
    corner_left = [wire("left", outl.at[ch], cr.at[ch]) for ch in range(4)]
    corner_right = [wire("right", outr.at[ch], cl.at[ch]) for ch in range(4)]
    w_steps = [wire("mate", w_rows, w_mate), wire("other", w_rows, w_other)]
    w_sides = [wire("left", w_pack, w_right), wire("right", w_pack, w_left)]
    for c in spots:
        c.start()
    for ch in VIA:
        via[ch].start()
    for ch in ORDER:
        if ch in direct:
            direct[ch].start()
        to_mate[ch].start()
        if ch % 2 == 0:
            to_left[ch // 2].start()
            to_right[ch // 2].start()
    loads[6].wait()
    w_rows[0:EDGE] = w[0:EDGE]
    w_rows[EDGE:] = w[CORE - EDGE :]
    for c in w_steps:
        c.start()

    sign = (1 - 2 * odd).astype(F32)
    block = (CORE, CORE)
    row = iota(block, 0).astype(F32) - (NEAR - 0.5)
    lane = iota(block, 1)
    sub = iota((EDGE, CORE), 0)
    nearer = lane < NEAR + q
    own_rows = row < p.astype(F32)

    def is_even(shape):
        return jnp.full(shape, odd, jnp.int32) == 0

    def forward_rows(channels):
        for ch in channels:
            to_mate[ch].got()
            if ch in relay:
                relay[ch].start()

    def forward_via(channels):
        for ch in channels:
            via[ch].got()
            across_via[ch].start()

    def forward_corners(channels):
        if 0 in channels:
            for c in spots:
                c.got()
        to_l = sign * (row - tall(place_l[...])) < 0
        to_r = sign * (row - tall(place_r[...])) < 0
        for ch in channels:
            {**direct, **across_via, **relay}[ch].got()
            m, n = mt[ch], nm[ch]
            outl[ch] = jnp.where(to_l, m, n)
            corner_left[ch].start()
            outr[ch] = jnp.where(to_r, m, n)
            corner_right[ch].start()

    mate_rows = sign * (row - p.astype(F32)) < 0

    def assemble(ch):
        if ch % 2 == 0:
            to_left[ch // 2].got()
            to_right[ch // 2].got()
        h = jnp.where(nearer, hr[ch], hl[ch])
        v = jnp.where(mate_rows, mt[ch], nm[ch])
        corner_left[ch].got()
        corner_right[ch].got()
        c = jnp.where(nearer, cr[ch], cl[ch])
        xs[ch] = cat(cat(tile[ch], h, 1), cat(v, c, 1), 0)

    loads[2].wait()
    loads[3].wait()
    phase = reorder(tab, phase_ref[...])
    kr, ki = jnp.cos(phase), jnp.sin(phase)
    loads[5].wait()
    turn_rows, turn_cols = p + (PROBE - HALO), q + (PROBE - HALO)
    pr, pi = (pltpu.roll(pltpu.roll(probe[n], turn_rows, 0), turn_cols, 1) for n in range(2))
    forward_via(VIA)
    forward_rows((0,))
    forward_corners((0,))
    loads[4].wait()
    measured = reorder(tab, amp[...])
    for ch in (1, 2, 3):
        forward_rows((ch,))
        forward_corners((ch,))
    assemble(0)
    assemble(1)
    ar, ai = xs[0], xs[1]
    fr, fi = forward(tab, ar * pr - ai * pi, ar * pi + ai * pr)
    wr, wi = inverse(tab, kr * fr - ki * fi, kr * fi + ki * fr)
    assemble(2)
    assemble(3)
    br, bi = xs[2], xs[3]
    fr, fi = forward(tab, br * wr - bi * wi, br * wi + bi * wr)
    for c in w_steps:
        c.got()
    thin = is_even((EDGE, CORE))
    below = jnp.where(thin, w_mate[0:EDGE], w_other[0:EDGE])
    above = jnp.where(thin, w_other[EDGE:], w_mate[EDGE:])
    w_edge = jnp.where(sub < EDGE // 2, below, above)
    w_pack[0:FOLD] = compact(squeeze(w[...], 0))
    w_pack[FOLD:] = squeeze(w_edge, 0)
    for c in w_sides:
        c.start()
    factor = 1.0 - measured * lax.rsqrt(fr * fr + fi * fi + AMP_EPS)
    gr_, gi_ = inverse(tab, fr * factor, fi * factor)

    across = {}
    lanes = iota((PROBE, CORE), 1)
    near_lanes = lanes < NEAR + q
    body_rows, rim_rows = pl.ds(0, CORE - 2 * EDGE), pl.ds(CORE - 2 * EDGE, PROBE - CORE + 2 * EDGE)

    def put(ch, grad):
        g[ch] = grad
        own, halo = grad[:, :CORE], grad[:, CORE:]
        to_r = jnp.where(lanes >= CORE - REACH, own, jnp.where(near_lanes, halo, 0.0))
        to_l = jnp.where(lanes < REACH, own, jnp.where(near_lanes, 0.0, halo))
        for n, (ref, x) in enumerate(((gr, to_r), (gl, to_l))):
            ref[ch] = cat_rows([x[EDGE:], x[:EDGE]])
        across[ch] = cross(ch, rim_rows)

    def cross(which, rows):
        pair = wire("right", gr.at[which, rows], il.at[which, rows]), wire("left", gl.at[which, rows], ir.at[which, rows])
        for c in pair:
            c.start()
        return pair

    upward, onward, beside, bridged = {}, {}, {}, {}

    lo, hi = CORE - STRIP, STRIP - EDGE

    def shares(first, last, down, up):
        even, thin = is_even(block), is_even((EDGE, CORE))
        rim = jnp.where(sub < REACH, down[:EDGE], jnp.where(sub >= EDGE - REACH, up[CORE - EDGE :], 0.0))
        up_far = cat_rows([up[:lo], jnp.where(sub < REACH, first, up[lo : lo + EDGE]), up[lo + EDGE :]])
        down_far = cat_rows([down[:hi], jnp.where(sub >= EDGE - REACH, last, down[hi : hi + EDGE]), down[hi + EDGE :]])
        far, near = jnp.where(even, up_far, down_far), jnp.where(even, down_far, up_far)
        mate_rim = jnp.where(thin, jnp.where(sub >= EDGE - REACH, last, 0.0), jnp.where(sub < REACH, first, 0.0))
        return rim, far, near, jnp.where(even, down, up), mate_rim

    bands = ((slice(0, EDGE), slice(PROBE - EDGE, PROBE)), (slice(CORE - EDGE, CORE), slice(CORE - 2 * EDGE, CORE - EDGE)))

    def joined(ch, mine, theirs):
        own, halo = g[ch, mine, :CORE], g[ch, mine, CORE:]
        fl, fr = il[ch, theirs], ir[ch, theirs]
        lane = iota(own.shape, 1)
        total = own + jnp.where(lane < CORE - REACH, fl, 0.0) + jnp.where(lane >= REACH, fr, 0.0)
        return total, halo + jnp.where(lane < REACH, fr, fl)

    packs = {}

    def fold(ch):
        s, n = divmod(ch, 2)
        for c in across[ch]:
            c.got()
        in_l = row < tall(place_l[...])
        in_r = row < tall(place_r[...])
        low = lane < REACH
        in_side = jnp.where(low, row - tall(place_r[...]), row - tall(place_l[...])) < 0
        far_rows = slice(CORE - EDGE, PROBE - EDGE)
        own, halo, fl, fr = g[ch, CORE:, :CORE], g[ch, CORE:, CORE:], il[ch, far_rows], ir[ch, far_rows]
        parts = ((own_rows, own), (in_l, jnp.where(lane < CORE - REACH, fl, 0.0)), (in_r, jnp.where(lane >= REACH, fr, 0.0)))
        down = sum(jnp.where(m, x, 0.0) for m, x in parts)
        up = sum(jnp.where(m, 0.0, x) for m, x in parts)
        ends = [joined(ch, *band) for band in bands]
        rim, far, near, base, mate_rim = shares(ends[0][0], ends[1][0], down, up)
        edge[ch], side_out[ch], near_out[ch] = rim, far, near
        strip = side_out.at[ch, high_strip], side_in.at[ch, high_strip]
        halves = [(side_out.at[ch, rows], side_in.at[ch, rows]) for rows in half_strips]
        near_strip = near_out.at[ch, low_strip], near_in.at[ch, low_strip]
        if ch in DIRECT_B:
            upward[ch] = wire("other", *strip)
            beside[ch] = wire("mate", *near_strip)
        else:
            upward[ch] = [wire("behind", *half) for half in halves]
            beside[ch] = wire("mate", *near_strip, jnp.logical_not(has["ahead"]), jnp.logical_not(has["other"]))
            mate_out[ch, :CORE], mate_out[ch, CORE:] = base, mate_rim
        for c in [upward[ch]] if ch in DIRECT_B else upward[ch]:
            c.start()
        beside[ch].start()
        o = jnp.where(low, fr, fl)
        pieces = [
            ends[0][1], ends[1][1],
            jnp.where(own_rows, halo, 0.0) + jnp.where(in_side, o, 0.0),
            jnp.where(own_rows, 0.0, halo) + jnp.where(in_side, 0.0, o),
        ]
        pieces = [squeeze(x, n) for x in pieces]
        if n == 0:
            packs[s] = pieces
            return
        pedge[s], far, near, _, _ = shares(*[a + b for a, b in zip(packs[s], pieces)])
        pside_out[s], pnear_out[s] = compact(far), compact(near)
        bridged[s] = wire("behind", pside_out.at[s], pbridge.at[s])
        upward[4 + s] = wire("mate", pbridge.at[s], pside_in.at[s], has["ahead"], has["other"])
        beside[4 + s] = wire("mate", pnear_out.at[s], pnear_in.at[s])
        bridged[s].start()
        beside[4 + s].start()

    def pass_pack(s):
        bridged[s].got()
        upward[4 + s].start()

    def fill(s):
        for c in inner[s]:
            c.got()
        for n in range(2):
            ch = 2 * s + n
            parts = [joined(ch, *bands[0])]
            parts.append(joined(ch, slice(EDGE, CORE - EDGE), slice(0, CORE - 2 * EDGE)))
            parts.append(joined(ch, *bands[1]))
            tot[ch] = cat_rows([x for x, _ in parts])
            margin = squeeze(cat_rows([x for _, x in parts]), n)
            ptot[s] = margin if n == 0 else ptot[s] + margin

    def incoming(x, turned=False):
        even, thin = is_even(block), is_even((EDGE, CORE))
        from_up, from_low = jnp.where(row < HALO - NEAR, x, 0.0), jnp.where(row > 0, x, 0.0)
        rim_low, rim_up = jnp.where(sub < REACH, x[lo : lo + EDGE], 0.0), jnp.where(sub >= EDGE - REACH, x[hi : hi + EDGE], 0.0)
        if turned:
            return jnp.where(even, from_up, from_low), jnp.where(thin, rim_up, rim_low)
        return jnp.where(even, from_low, from_up), jnp.where(thin, rim_low, rim_up)

    def pass_on(ch):
        onward[ch] = []
        for n, rows in enumerate((pl.ds(0, CUT), pl.ds(CUT, TVROWS - CUT))):
            upward[ch][n].got()
            if n == 0:
                x = side_in[ch, :CUT]
                mate_out[ch, :CUT] += jnp.where(is_even(x.shape), jnp.where(row[:CUT] > 0, x, 0.0), x)
            else:
                more, rim = incoming(side_in[ch])
                mate_out[ch, CUT:CORE] += more[CUT:]
                mate_out[ch, CORE:] += rim
            onward[ch].append(wire("mate", mate_out.at[ch, rows], mate_in.at[ch, rows], has["ahead"], has["other"]))
            onward[ch][n].start()

    def total(ch):
        beside[ch].got()
        a, ra = incoming(near_in[ch])
        if ch in DIRECT_B:
            upward[ch].got()
            b, rb = incoming(side_in[ch], True)
        else:
            for c in onward[ch]:
                c.got()
            b, rb = mate_in[ch, :CORE], mate_in[ch, CORE:]
        return cat_rows([a + b, ra + rb])

    shape = (TVROWS, PROBE)

    def prepare(s):
        rest = cat_rows([ptot[s], pedge[s]])
        for n in range(2):
            ch = 2 * s + n
            grad = cat(cat_rows([tot[ch], edge[ch]]), pltpu.roll(rest, CORE - REACH - 8 * n, 1), 1)
            wide = iota((EDGE, PROBE), 0) < EDGE // 2
            rim = jnp.where(wide, xs[ch, CORE : CORE + EDGE, :], xs[ch, PROBE - EDGE :, :])
            fields[ch] = (cat_rows([xs[ch, :CORE, :], rim]) - LEARN_RATE * grad) * inside

    def smooth(s):
        upward[4 + s].got()
        beside[4 + s].got()
        (a, ra), (b, rb) = incoming(expand(pnear_in[s])), incoming(expand(pside_in[s]), True)
        rest = cat_rows([a + b, ra + rb])
        pair = []
        for n in range(2):
            ch = 2 * s + n
            grad = cat(total(ch), pltpu.roll(rest, CORE - REACH - 8 * n, 1), 1)
            pair.append(fields[ch] - LEARN_RATE * inside * grad)
        for _ in range(TV_STEPS):
            down = [pltpu.roll(f, TVROWS - 1, 0) - f for f in pair]
            along_row = [pltpu.roll(f, PROBE - 1, 1) - f for f in pair]
            square = down[0] * down[0] + along_row[0] * along_row[0] + (down[1] * down[1] + along_row[1] * along_row[1])
            gain = weight * lax.rsqrt(square + TV_EPS)
            fresh = []
            for f, d, r in zip(pair, down, along_row):
                d, r = gain * d, gain * r
                update = d - pltpu.roll(d, 1, 0) + (r - pltpu.roll(r, 1, 1))
                fresh.append((f + TV_TAU * update) * inside)
            pair = fresh
        for n in range(2):
            out[2 * s + n] = pair[n][:CORE, :CORE]

    put(2, wr * gr_ + wi * gi_)
    put(3, wr * gi_ - wi * gr_)
    fr, fi = forward(tab, br * gr_ + bi * gi_, br * gi_ - bi * gr_)
    gr_, gi_ = inverse(tab, kr * fr + ki * fi, kr * fi - ki * fr)
    put(0, pr * gr_ + pi * gi_)
    put(1, pr * gi_ - pi * gr_)
    inner = {s: cross(pl.ds(2 * s, 2), body_rows) for s in (1, 0)}
    fold(2)
    fold(3)
    for c in w_sides:
        c.got()
    row_at, col_at = iota(shape, 0), iota(shape, 1)
    row_at = place.r * CORE + jnp.where(row_at < CORE + EDGE // 2, row_at, row_at - TVROWS)
    col_at = place.c * CORE + jnp.where(col_at < CORE + HALF // 2, col_at, col_at - PROBE)
    inside = (row_at >= 0) & (row_at < place.nr * CORE) & (col_at >= 0) & (col_at < place.nc * CORE)
    inside = inside.astype(F32)
    margins = [cat_rows([expand(ref[:FOLD]), ref[FOLD:]]) for ref in (w_right, w_left)]
    margins = [pltpu.roll(m, CORE - REACH, 1) for m in margins]
    far = jnp.where(iota((TVROWS, CORE), 1) < HALF // 2, margins[0], margins[1])
    weight = cat(cat_rows([w[...], w_edge]), far, 1) * inside
    fold(0)
    fold(1)
    pass_on(2)
    pass_pack(1)
    pass_on(0)
    pass_pack(0)
    fill(1)
    prepare(1)
    fill(0)
    prepare(0)
    smooth(1)
    smooth(0)
    assert wire.count == COPIES
    for c in wire.all:
        c.sent()


COPIES = 60
CUT = 56
ORDER = (0, 1, 2, 3)
DIRECT_A = (0, 1)
VIA = (2, 3)
DIRECT_B = (1, 3)


def body(transmission, probe, fresnel_phase, amplitudes, positions, tv_weight):
    vmem, anywhere = (pl.BlockSpec(memory_space=m) for m in (pltpu.VMEM, pl.ANY))
    tab = tables()

    def scratch(*shape):
        return pltpu.VMEM(shape, F32)

    four = lambda n: [scratch(4, CORE, CORE)] * n
    small = lambda n: [scratch(EDGE, CORE)] * n
    out = pl.pallas_call(
        whole_kernel,
        out_shape=pltpu.VMEM((4, CORE, CORE), F32),
        in_specs=[anywhere] * 7,
        out_specs=vmem,
        scratch_shapes=[
            pltpu.SMEM((2,), jnp.int32), scratch(4, CORE, CORE), scratch(CORE, CORE), scratch(2, PROBE, PROBE),
            scratch(PROBE, PROBE), scratch(PROBE, PROBE), pltpu.VMEM(tab.shape, BF16),
            *four(9), *small(3), scratch(4, PROBE, PROBE),
            *[scratch(2 * EDGE, CORE)] * 3, *[scratch(FOLD + EDGE, CORE)] * 3,
            scratch(4, PROBE, PROBE), *[scratch(4, PROBE, CORE)] * 4,
            scratch(4, CORE, CORE), scratch(4, EDGE, CORE), *four(4), *[scratch(4, TVROWS, CORE)] * 2,
            scratch(4, TVROWS, PROBE), scratch(2, CORE, CORE), scratch(2, EDGE, CORE), *[scratch(2, FOLD, CORE)] * 5,
            pltpu.SemaphoreType.DMA((len(OPPOSITE),)),
            pltpu.SemaphoreType.DMA((COPIES,)),
            pltpu.SemaphoreType.DMA((7,)),
        ],
        compiler_params=pltpu.CompilerParams(collective_id=0, has_side_effects=True),
        name="ptycho",
    )(
        positions.reshape(2), transmission.reshape(4, CORE, CORE), tv_weight, probe, fresnel_phase,
        amplitudes.reshape(PROBE, PROBE), jnp.asarray(tab),
    )
    return out.reshape(2, 2, CORE, CORE)


def solution(mesh):
    placed = (
        P(None, None, "row", "col"),
        P(),
        P(),
        P("row", "col", None, None, None),
        P("row", "col", None, None),
        P("row", "col"),
    )
    return jax.shard_map(
        body, mesh=mesh, in_specs=placed, out_specs=P(None, None, "row", "col"), check_vma=False
    )
```

```python
import functools
import math

import jax
import jax.numpy as jnp
import numpy as np
from jax import lax
from jax.experimental import pallas as pl
from jax.experimental.pallas import tpu as pltpu
from jax.sharding import PartitionSpec as P

MESH = pl.DeviceIdType.MESH
F32, BF16 = jnp.float32, jnp.bfloat16
CORE = 128
PROBE = 256
HALF = 128
HALO = 100
NEAR = PROBE - CORE - HALO
STRIP = 104
REACH = 3
EDGE = 8
TVROWS = CORE + EDGE
FOLD = 16
AMP_EPS = 0.1
LEARN_RATE = 0.2
TV_EPS = 1.0
TV_TAU = 0.1
TV_STEPS = 3


def tables():
    k, j = np.arange(HALF)[:, None], np.arange(HALF)[None, :]
    parts = []
    for odd in (0, 1):
        angle = 2.0 * np.pi * (((2 * k + odd) * j) % PROBE) / PROBE
        c, s = np.cos(angle) / math.sqrt(PROBE), np.sin(angle) / math.sqrt(PROBE)
        full = np.block([[c, s], [-s, c]])
        parts.append(full)
    out = []
    for full in (parts[0], parts[0].T, parts[1], parts[1].T):
        full = full.astype(np.float32)
        high = full.astype(BF16)
        out += [high, (full - high.astype(np.float32)).astype(BF16)]
    order = np.zeros((PROBE, PROBE), np.float32)
    order[np.arange(HALF), 2 * np.arange(HALF)] = 1
    order[HALF + np.arange(HALF), 2 * np.arange(HALF) + 1] = 1
    out += [order.astype(BF16), order.T.astype(BF16)]
    return np.stack(out)


def split(x):
    high = x.astype(BF16)
    return high, (x - high.astype(F32)).astype(BF16)


def mm(a, b):
    return jnp.dot(a, b, preferred_element_type=F32)


def left(tab, i, x):
    wh, wl = tab[2 * i], tab[2 * i + 1]
    xh, xl = split(x)
    return mm(wh, xh) + (mm(wh, xl) + mm(wl, xh))


def right(tab, i, x):
    wh, wl = tab[2 * i], tab[2 * i + 1]
    xh, xl = split(x)
    return mm(xh, wh) + (mm(xl, wh) + mm(xh, wl))


def cat(a, b, axis):
    return jnp.concatenate([a, b], axis=axis)


def forward(tab, re, im):
    h = HALF
    e = left(tab, 0, cat(re[:h] + re[h:], im[:h] + im[h:], 0))
    o = left(tab, 2, cat(re[:h] - re[h:], im[:h] - im[h:], 0))
    re, im = cat(e[:h], o[:h], 0), cat(e[h:], o[h:], 0)
    e = right(tab, 1, cat(re[:, :h] + re[:, h:], im[:, :h] + im[:, h:], 1))
    o = right(tab, 3, cat(re[:, :h] - re[:, h:], im[:, :h] - im[:, h:], 1))
    return cat(e[:, :h], o[:, :h], 1), cat(e[:, h:], o[:, h:], 1)


def inverse(tab, re, im):
    h = HALF
    e = left(tab, 1, cat(re[:h], im[:h], 0))
    o = left(tab, 3, cat(re[h:], im[h:], 0))
    s, d = e + o, e - o
    re, im = cat(s[:h], d[:h], 0), cat(s[h:], d[h:], 0)
    e = right(tab, 0, cat(re[:, :h], im[:, :h], 1))
    o = right(tab, 2, cat(re[:, h:], im[:, h:], 1))
    s, d = e + o, e - o
    return cat(s[:, :h], d[:, :h], 1), cat(s[:, h:], d[:, h:], 1)


def reorder(tab, x):
    for axis in (0, 1):
        total = None
        rest = x
        for _ in range(3):
            part = rest.astype(BF16)
            rest = rest - part.astype(F32)
            term = mm(tab[8], part) if axis == 0 else mm(part, tab[9])
            total = term if total is None else total + term
        x = total
    return x


class Place:
    def __init__(self):
        self.r, self.c = lax.axis_index("row"), lax.axis_index("col")
        self.nr, self.nc = lax.axis_size("row"), lax.axis_size("col")
        self.odd = lax.rem(self.r, 2)
        step = 1 - 2 * self.odd
        rows = {"mate": self.r + step, "other": self.r - step, "ahead": self.r + 2 * step, "behind": self.r - 2 * step}
        self.to = {side: {"row": at} for side, at in rows.items()}
        self.has = {side: (at >= 0) & (at < self.nr) for side, at in rows.items()}
        for side, at in (("left", self.c - 1), ("right", self.c + 1)):
            self.to[side] = {"col": at}
            self.has[side] = (at >= 0) & (at < self.nc)

    def signal(self):
        sem = pltpu.get_barrier_semaphore()
        for side in OPPOSITE:
            @pl.when(self.has[side])
            def _():
                pl.semaphore_signal(sem, inc=1, device_id=self.to[side], device_id_type=MESH)

    def wait(self):
        sem = pltpu.get_barrier_semaphore()
        pl.semaphore_wait(sem, sum(self.has[side].astype(jnp.int32) for side in OPPOSITE))


OPPOSITE = {"left": "right", "right": "left", "mate": "mate", "other": "other", "ahead": "behind", "behind": "ahead"}


class Wire:
    def __init__(self, place, send, recv):
        self.place, self.send, self.recv = place, send, recv
        self.count, self.all = 0, []

    def __call__(self, side, src, dst, sends=True, gets=True):
        copy = Copy(self.place, side, src, dst, self.send.at[list(OPPOSITE).index(side)], self.recv.at[self.count])
        copy.sends, copy.gets = copy.sends & sends, copy.gets & gets
        self.count += 1
        self.all.append(copy)
        return copy


class Copy:
    def __init__(self, place, side, src, dst, send, recv):
        self.op = pltpu.make_async_remote_copy(
            src_ref=src, dst_ref=dst, send_sem=send, recv_sem=recv, device_id=place.to[side], device_id_type=MESH,
        )
        self.sends, self.gets = place.has[side], place.has[OPPOSITE[side]]

    def start(self):
        pl.when(self.sends)(lambda: self.op.start())

    def got(self):
        pl.when(self.gets)(lambda: self.op.wait_recv())

    def sent(self):
        pl.when(self.sends)(lambda: self.op.wait_send())


def iota(shape, axis):
    return lax.broadcasted_iota(jnp.int32, shape, axis)


def tall(tile):
    return cat_rows([tile] * (CORE // EDGE))


def cat_rows(parts):
    return jnp.concatenate(parts, axis=0)


def compact(x):
    parts = [x[FOLD * k : FOLD * k + FOLD] for k in range(CORE // FOLD)]
    return parts[0] + sum(pltpu.roll(part, FOLD * k, 1) for k, part in enumerate(parts) if k)


def expand(x):
    return cat_rows([x] + [pltpu.roll(x, CORE - FOLD * k, 1) for k in range(1, CORE // FOLD)])


def squeeze(x, n):
    lane = iota(x.shape, 1)
    x = jnp.where((lane < REACH) | (lane >= CORE - REACH), x, 0.0)
    return pltpu.roll(x, REACH + 8 * n, 1)


def whole_kernel(
    pos_any, tr_any, w_any, probe_any, phase_any, amp_any, tab_any, out,
    pos, tile, w, probe, phase_ref, amp, tab,
    hl, hr, cl, cr, mt, nm, bridge, outl, outr, place_me, place_l, place_r, xs,
    w_rows, w_mate, w_other, w_pack, w_left, w_right,
    g, gl, gr, il, ir, tot, edge, side_out, side_in, near_out, near_in, mate_out, mate_in,
    fields, ptot, pedge, pbridge, pside_out, pside_in, pnear_out, pnear_in,
    send, recv, local,
):
    place = Place()
    has, odd = place.has, place.odd
    place.signal()
    loads = []
    pairs = (
        (tr_any, tile), (pos_any, pos), (phase_any, phase_ref), (tab_any, tab), (amp_any, amp), (probe_any, probe), (w_any, w),
    )
    for n, (src, dst) in enumerate(pairs):
        load = pltpu.make_async_copy(src, dst, local.at[n])
        load.start()
        loads.append(load)
    wire = Wire(place, send, recv)
    for side, refs in (
        ("left", (hl, cl, il, place_l, w_left)), ("right", (hr, cr, ir, place_r, w_right)),
        ("other", (nm, w_other, pside_in, *(side_in.at[ch] for ch in DIRECT_B), *(mate_in.at[ch] for ch in range(4) if ch not in DIRECT_B))),
        ("ahead", tuple(side_in.at[ch] for ch in range(4) if ch not in DIRECT_B)),
    ):
        @pl.when(jnp.logical_not(has[side]))
        def _():
            for ref in refs:
                ref[...] = jnp.zeros(ref.shape, F32)

    @pl.when(has["other"])
    def _():
        for ch in range(4):
            if ch not in DIRECT_B:
                near_in[ch] = jnp.zeros((CORE, CORE), F32)

    loads[1].wait()
    p, q = pos[0], pos[1]
    place_me[...] = jnp.full((EDGE, CORE), p.astype(F32))
    loads[0].wait()
    place.wait()

    low_strip = pl.ds(pl.multiple_of((CORE - STRIP) * odd, EDGE), STRIP)
    high_strip = pl.ds(pl.multiple_of((CORE - STRIP) * (1 - odd), EDGE), STRIP)
    half_strips = [
        pl.ds(pl.multiple_of((CORE - STRIP) * (1 - odd) + at, EDGE), size) for at, size in ((0, CUT), (CUT, STRIP - CUT))
    ]
    direct = {ch: wire("other", tile.at[ch, low_strip], nm.at[ch, low_strip]) for ch in DIRECT_A}
    to_mate = [
        wire("mate", *(ref.at[ch, high_strip if ch in (*direct, *VIA) else pl.ds(0, CORE)] for ref in (tile, mt))) for ch in range(4)
    ]
    slices = [pl.ds(2 * s, 2) for s in range(2)]
    to_left = [wire("left", tile.at[part], hr.at[part]) for part in slices]
    to_right = [wire("right", tile.at[part], hl.at[part]) for part in slices]
    via = {ch: wire("behind", tile.at[ch, low_strip], bridge.at[ch, low_strip]) for ch in VIA}
    across_via = {
        ch: wire("mate", bridge.at[ch, low_strip], nm.at[ch, low_strip], has["ahead"], has["other"]) for ch in VIA
    }
    relay = {
        ch: wire("ahead", mt.at[ch, high_strip], nm.at[ch, high_strip]) for ch in range(4) if ch not in (*direct, *via)
    }
    spots = [wire("left", place_me, place_r), wire("right", place_me, place_l)]
    corner_left = [wire("left", outl.at[ch], cr.at[ch]) for ch in range(4)]
    corner_right = [wire("right", outr.at[ch], cl.at[ch]) for ch in range(4)]
    w_steps = [wire("mate", w_rows, w_mate), wire("other", w_rows, w_other)]
    w_sides = [wire("left", w_pack, w_right), wire("right", w_pack, w_left)]
    for c in spots:
        c.start()
    for ch in VIA:
        via[ch].start()
    for ch in ORDER:
        if ch in direct:
            direct[ch].start()
        to_mate[ch].start()
        if ch % 2 == 0:
            to_left[ch // 2].start()
            to_right[ch // 2].start()
    loads[6].wait()
    w_rows[0:EDGE] = w[0:EDGE]
    w_rows[EDGE:] = w[CORE - EDGE :]
    for c in w_steps:
        c.start()

    sign = (1 - 2 * odd).astype(F32)
    block = (CORE, CORE)
    row = iota(block, 0).astype(F32) - (NEAR - 0.5)
    lane = iota(block, 1)
    sub = iota((EDGE, CORE), 0)
    nearer = lane < NEAR + q
    own_rows = row < p.astype(F32)

    def is_even(shape):
        return jnp.full(shape, odd, jnp.int32) == 0

    def forward_rows(channels):
        for ch in channels:
            to_mate[ch].got()
            if ch in relay:
                relay[ch].start()

    def forward_via(channels):
        for ch in channels:
            via[ch].got()
            across_via[ch].start()

    def forward_corners(channels):
        if 0 in channels:
            for c in spots:
                c.got()
        to_l = sign * (row - tall(place_l[...])) < 0
        to_r = sign * (row - tall(place_r[...])) < 0
        for ch in channels:
            {**direct, **across_via, **relay}[ch].got()
            m, n = mt[ch], nm[ch]
            outl[ch] = jnp.where(to_l, m, n)
            corner_left[ch].start()
            outr[ch] = jnp.where(to_r, m, n)
            corner_right[ch].start()

    mate_rows = sign * (row - p.astype(F32)) < 0

    def assemble(ch):
        if ch % 2 == 0:
            to_left[ch // 2].got()
            to_right[ch // 2].got()
        h = jnp.where(nearer, hr[ch], hl[ch])
        v = jnp.where(mate_rows, mt[ch], nm[ch])
        corner_left[ch].got()
        corner_right[ch].got()
        c = jnp.where(nearer, cr[ch], cl[ch])
        xs[ch] = cat(cat(tile[ch], h, 1), cat(v, c, 1), 0)

    loads[2].wait()
    loads[3].wait()
    phase = reorder(tab, phase_ref[...])
    kr, ki = jnp.cos(phase), jnp.sin(phase)
    loads[5].wait()
    turn_rows, turn_cols = p + (PROBE - HALO), q + (PROBE - HALO)
    pr, pi = (pltpu.roll(pltpu.roll(probe[n], turn_rows, 0), turn_cols, 1) for n in range(2))
    forward_via(VIA)
    forward_rows((0,))
    forward_corners((0,))
    loads[4].wait()
    measured = reorder(tab, amp[...])
    for ch in (1, 2, 3):
        forward_rows((ch,))
        forward_corners((ch,))
    assemble(0)
    assemble(1)
    ar, ai = xs[0], xs[1]
    fr, fi = forward(tab, ar * pr - ai * pi, ar * pi + ai * pr)
    wr, wi = inverse(tab, kr * fr - ki * fi, kr * fi + ki * fr)
    assemble(2)
    assemble(3)
    br, bi = xs[2], xs[3]
    fr, fi = forward(tab, br * wr - bi * wi, br * wi + bi * wr)
    for c in w_steps:
        c.got()
    thin = is_even((EDGE, CORE))
    below = jnp.where(thin, w_mate[0:EDGE], w_other[0:EDGE])
    above = jnp.where(thin, w_other[EDGE:], w_mate[EDGE:])
    w_edge = jnp.where(sub < EDGE // 2, below, above)
    w_pack[0:FOLD] = compact(squeeze(w[...], 0))
    w_pack[FOLD:] = squeeze(w_edge, 0)
    for c in w_sides:
        c.start()
    factor = 1.0 - measured * lax.rsqrt(fr * fr + fi * fi + AMP_EPS)
    gr_, gi_ = inverse(tab, fr * factor, fi * factor)

    across = {}
    lanes = iota((PROBE, CORE), 1)
    near_lanes = lanes < NEAR + q
    body_rows, rim_rows = pl.ds(0, CORE - 2 * EDGE), pl.ds(CORE - 2 * EDGE, PROBE - CORE + 2 * EDGE)

    def put(ch, grad):
        g[ch] = grad
        own, halo = grad[:, :CORE], grad[:, CORE:]
        to_r = jnp.where(lanes >= CORE - REACH, own, jnp.where(near_lanes, halo, 0.0))
        to_l = jnp.where(lanes < REACH, own, jnp.where(near_lanes, 0.0, halo))
        for n, (ref, x) in enumerate(((gr, to_r), (gl, to_l))):
            ref[ch] = cat_rows([x[EDGE:], x[:EDGE]])
        across[ch] = cross(ch, rim_rows)

    def cross(which, rows):
        pair = wire("right", gr.at[which, rows], il.at[which, rows]), wire("left", gl.at[which, rows], ir.at[which, rows])
        for c in pair:
            c.start()
        return pair

    upward, onward, beside, bridged = {}, {}, {}, {}

    lo, hi = CORE - STRIP, STRIP - EDGE

    def shares(first, last, down, up):
        even, thin = is_even(block), is_even((EDGE, CORE))
        rim = jnp.where(sub < REACH, down[:EDGE], jnp.where(sub >= EDGE - REACH, up[CORE - EDGE :], 0.0))
        up_far = cat_rows([up[:lo], jnp.where(sub < REACH, first, up[lo : lo + EDGE]), up[lo + EDGE :]])
        down_far = cat_rows([down[:hi], jnp.where(sub >= EDGE - REACH, last, down[hi : hi + EDGE]), down[hi + EDGE :]])
        far, near = jnp.where(even, up_far, down_far), jnp.where(even, down_far, up_far)
        mate_rim = jnp.where(thin, jnp.where(sub >= EDGE - REACH, last, 0.0), jnp.where(sub < REACH, first, 0.0))
        return rim, far, near, jnp.where(even, down, up), mate_rim

    bands = ((slice(0, EDGE), slice(PROBE - EDGE, PROBE)), (slice(CORE - EDGE, CORE), slice(CORE - 2 * EDGE, CORE - EDGE)))

    def joined(ch, mine, theirs):
        own, halo = g[ch, mine, :CORE], g[ch, mine, CORE:]
        fl, fr = il[ch, theirs], ir[ch, theirs]
        lane = iota(own.shape, 1)
        total = own + jnp.where(lane < CORE - REACH, fl, 0.0) + jnp.where(lane >= REACH, fr, 0.0)
        return total, halo + jnp.where(lane < REACH, fr, fl)

    packs = {}

    def fold(ch):
        s, n = divmod(ch, 2)
        for c in across[ch]:
            c.got()
        in_l = row < tall(place_l[...])
        in_r = row < tall(place_r[...])
        low = lane < REACH
        in_side = jnp.where(low, row - tall(place_r[...]), row - tall(place_l[...])) < 0
        far_rows = slice(CORE - EDGE, PROBE - EDGE)
        own, halo, fl, fr = g[ch, CORE:, :CORE], g[ch, CORE:, CORE:], il[ch, far_rows], ir[ch, far_rows]
        parts = ((own_rows, own), (in_l, jnp.where(lane < CORE - REACH, fl, 0.0)), (in_r, jnp.where(lane >= REACH, fr, 0.0)))
        down = sum(jnp.where(m, x, 0.0) for m, x in parts)
        up = sum(jnp.where(m, 0.0, x) for m, x in parts)
        ends = [joined(ch, *band) for band in bands]
        rim, far, near, base, mate_rim = shares(ends[0][0], ends[1][0], down, up)
        edge[ch], side_out[ch], near_out[ch] = rim, far, near
        strip = side_out.at[ch, high_strip], side_in.at[ch, high_strip]
        halves = [(side_out.at[ch, rows], side_in.at[ch, rows]) for rows in half_strips]
        near_strip = near_out.at[ch, low_strip], near_in.at[ch, low_strip]
        if ch in DIRECT_B:
            upward[ch] = wire("other", *strip)
            beside[ch] = wire("mate", *near_strip)
        else:
            upward[ch] = [wire("behind", *half) for half in halves]
            beside[ch] = wire("mate", *near_strip, jnp.logical_not(has["ahead"]), jnp.logical_not(has["other"]))
            mate_out[ch, :CORE], mate_out[ch, CORE:] = base, mate_rim
        for c in [upward[ch]] if ch in DIRECT_B else upward[ch]:
            c.start()
        beside[ch].start()
        o = jnp.where(low, fr, fl)
        pieces = [
            ends[0][1], ends[1][1],
            jnp.where(own_rows, halo, 0.0) + jnp.where(in_side, o, 0.0),
            jnp.where(own_rows, 0.0, halo) + jnp.where(in_side, 0.0, o),
        ]
        pieces = [squeeze(x, n) for x in pieces]
        if n == 0:
            packs[s] = pieces
            return
        pedge[s], far, near, _, _ = shares(*[a + b for a, b in zip(packs[s], pieces)])
        pside_out[s], pnear_out[s] = compact(far), compact(near)
        bridged[s] = wire("behind", pside_out.at[s], pbridge.at[s])
        upward[4 + s] = wire("mate", pbridge.at[s], pside_in.at[s], has["ahead"], has["other"])
        beside[4 + s] = wire("mate", pnear_out.at[s], pnear_in.at[s])
        bridged[s].start()
        beside[4 + s].start()

    def pass_pack(s):
        bridged[s].got()
        upward[4 + s].start()

    def fill(s):
        for c in inner[s]:
            c.got()
        for n in range(2):
            ch = 2 * s + n
            parts = [joined(ch, *bands[0])]
            parts.append(joined(ch, slice(EDGE, CORE - EDGE), slice(0, CORE - 2 * EDGE)))
            parts.append(joined(ch, *bands[1]))
            tot[ch] = cat_rows([x for x, _ in parts])
            margin = squeeze(cat_rows([x for _, x in parts]), n)
            ptot[s] = margin if n == 0 else ptot[s] + margin

    def incoming(x, turned=False):
        even, thin = is_even(block), is_even((EDGE, CORE))
        from_up, from_low = jnp.where(row < HALO - NEAR, x, 0.0), jnp.where(row > 0, x, 0.0)
        rim_low, rim_up = jnp.where(sub < REACH, x[lo : lo + EDGE], 0.0), jnp.where(sub >= EDGE - REACH, x[hi : hi + EDGE], 0.0)
        if turned:
            return jnp.where(even, from_up, from_low), jnp.where(thin, rim_up, rim_low)
        return jnp.where(even, from_low, from_up), jnp.where(thin, rim_low, rim_up)

    def pass_on(ch):
        onward[ch] = []
        for n, rows in enumerate((pl.ds(0, CUT), pl.ds(CUT, TVROWS - CUT))):
            upward[ch][n].got()
            if n == 0:
                x = side_in[ch, :CUT]
                mate_out[ch, :CUT] += jnp.where(is_even(x.shape), jnp.where(row[:CUT] > 0, x, 0.0), x)
            else:
                more, rim = incoming(side_in[ch])
                mate_out[ch, CUT:CORE] += more[CUT:]
                mate_out[ch, CORE:] += rim
            onward[ch].append(wire("mate", mate_out.at[ch, rows], mate_in.at[ch, rows], has["ahead"], has["other"]))
            onward[ch][n].start()

    def total(ch):
        beside[ch].got()
        a, ra = incoming(near_in[ch])
        if ch in DIRECT_B:
            upward[ch].got()
            b, rb = incoming(side_in[ch], True)
        else:
            for c in onward[ch]:
                c.got()
            b, rb = mate_in[ch, :CORE], mate_in[ch, CORE:]
        return cat_rows([a + b, ra + rb])


    slab = (TVROWS, CORE)
    turn = CORE // 2

    def both(first, second):
        at = iota(slab, 1)
        return jnp.where((at >= turn // 2) & (at < turn + turn // 2), second, first)

    def unpack(rest):
        return both(pltpu.roll(rest, CORE - REACH, 1), pltpu.roll(rest, turn - REACH - 8, 1))

    def kept(x):
        return cat_rows([x[:CORE], x[CORE:] * in_rim])

    def prepare(s):
        sides = []
        for n in range(2):
            ch = 2 * s + n
            wide = iota((EDGE, PROBE), 0) < EDGE // 2
            rim = jnp.where(wide, xs[ch, CORE : CORE + EDGE, :], xs[ch, PROBE - EDGE :, :])
            grad = cat_rows([tot[ch], edge[ch]])
            fields[s, n] = kept(cat_rows([xs[ch, :CORE, :CORE], rim[:, :CORE]]) - LEARN_RATE * grad)
            sides.append(cat_rows([xs[ch, :CORE, CORE:], rim[:, CORE:]]))
        side = both(sides[0], pltpu.roll(sides[1], turn, 1))
        fields[s, 2] = (side - LEARN_RATE * unpack(cat_rows([ptot[s], pedge[s]]))) * side_inside

    def smooth(s):
        upward[4 + s].got()
        beside[4 + s].got()
        (a, ra), (b, rb) = incoming(expand(pnear_in[s])), incoming(expand(pside_in[s]), True)
        side = fields[s, 2] - LEARN_RATE * side_inside * unpack(cat_rows([a + b, ra + rb]))
        own = [fields[s, n] - LEARN_RATE * kept(total(2 * s + n)) for n in range(2)]
        at = iota(slab, 1)
        first, last = at == 0, at == CORE - 1
        for _ in range(TV_STEPS):
            three = (*own, side)
            after = [pltpu.roll(f, CORE - 1, 1) for f in three]
            right = [
                jnp.where(last, after[2], after[0]),
                jnp.where(last, pltpu.roll(side, turn - 1, 1), after[1]),
                jnp.where(last, after[0], jnp.where(at == turn - 1, pltpu.roll(own[1], turn - 1, 1), after[2])),
            ]
            right = [x - f for x, f in zip(right, three)]
            down = [pltpu.roll(f, TVROWS - 1, 0) - f for f in three]
            squares = [d * d + r * r for d, r in zip(down, right)]
            gain = weight * lax.rsqrt(squares[0] + squares[1] + TV_EPS)
            side_gain = side_weight * lax.rsqrt(squares[2] + pltpu.roll(squares[2], turn, 1) + TV_EPS)
            gains = (gain, gain, side_gain)
            down = [k * d for k, d in zip(gains, down)]
            right = [k * r for k, r in zip(gains, right)]
            before = [pltpu.roll(r, 1, 1) for r in right]
            left = [
                jnp.where(first, before[2], before[0]),
                jnp.where(first, pltpu.roll(right[2], turn + 1, 1), before[1]),
                jnp.where(first, before[0], jnp.where(at == turn, pltpu.roll(right[1], turn + 1, 1), before[2])),
            ]
            fresh = [
                f + (d - pltpu.roll(d, 1, 0) + (r - x)) for f, d, r, x in zip(three, down, right, left)
            ]
            own, side = [kept(f) for f in fresh[:2]], fresh[2] * side_inside
        for n in range(2):
            out[2 * s + n] = own[n][:CORE]

    put(2, wr * gr_ + wi * gi_)
    put(3, wr * gi_ - wi * gr_)
    fr, fi = forward(tab, br * gr_ + bi * gi_, br * gi_ - bi * gr_)
    gr_, gi_ = inverse(tab, kr * fr + ki * fi, kr * fi - ki * fr)
    put(0, pr * gr_ + pi * gi_)
    put(1, pr * gi_ - pi * gr_)
    inner = {s: cross(pl.ds(2 * s, 2), body_rows) for s in (1, 0)}
    fold(2)
    fold(3)
    for c in w_sides:
        c.got()
    row_at, col_at = iota(slab, 0), iota(slab, 1)
    row_at = place.r * CORE + jnp.where(row_at < CORE + EDGE // 2, row_at, row_at - TVROWS)
    col_at = both(col_at, col_at - turn + jnp.where(col_at < turn, CORE, 0))
    col_at = place.c * CORE + jnp.where(col_at < turn, col_at + CORE, col_at - CORE)
    in_rows = (row_at >= 0) & (row_at < place.nr * CORE)
    side_inside = (in_rows & (col_at >= 0) & (col_at < place.nc * CORE)).astype(F32)
    in_rim = in_rows.astype(F32)[CORE:]
    margins = [cat_rows([expand(ref[:FOLD]), ref[FOLD:]]) for ref in (w_right, w_left)]
    margins = [pltpu.roll(m, CORE - REACH, 1) for m in margins]
    far = jnp.where(iota(slab, 1) < turn, margins[0], margins[1])
    weight = TV_TAU * kept(cat_rows([w[...], w_edge]))
    side_weight = TV_TAU * side_inside * both(far, pltpu.roll(far, turn, 1))
    fold(0)
    fold(1)
    pass_on(2)
    pass_pack(1)
    pass_on(0)
    pass_pack(0)
    fill(1)
    prepare(1)
    fill(0)
    prepare(0)
    smooth(1)
    smooth(0)
    assert wire.count == COPIES
    for c in wire.all:
        c.sent()


COPIES = 60
CUT = 56
ORDER = (0, 1, 2, 3)
DIRECT_A = (0, 1)
VIA = (2, 3)
DIRECT_B = (1, 3)


def body(transmission, probe, fresnel_phase, amplitudes, positions, tv_weight):
    vmem, anywhere = (pl.BlockSpec(memory_space=m) for m in (pltpu.VMEM, pl.ANY))
    tab = tables()

    def scratch(*shape):
        return pltpu.VMEM(shape, F32)

    four = lambda n: [scratch(4, CORE, CORE)] * n
    small = lambda n: [scratch(EDGE, CORE)] * n
    out = pl.pallas_call(
        whole_kernel,
        out_shape=pltpu.VMEM((4, CORE, CORE), F32),
        in_specs=[anywhere] * 7,
        out_specs=vmem,
        scratch_shapes=[
            pltpu.SMEM((2,), jnp.int32), scratch(4, CORE, CORE), scratch(CORE, CORE), scratch(2, PROBE, PROBE),
            scratch(PROBE, PROBE), scratch(PROBE, PROBE), pltpu.VMEM(tab.shape, BF16),
            *four(9), *small(3), scratch(4, PROBE, PROBE),
            *[scratch(2 * EDGE, CORE)] * 3, *[scratch(FOLD + EDGE, CORE)] * 3,
            scratch(4, PROBE, PROBE), *[scratch(4, PROBE, CORE)] * 4,
            scratch(4, CORE, CORE), scratch(4, EDGE, CORE), *four(4), *[scratch(4, TVROWS, CORE)] * 2,
            scratch(2, 3, TVROWS, CORE), scratch(2, CORE, CORE), scratch(2, EDGE, CORE), *[scratch(2, FOLD, CORE)] * 5,
            pltpu.SemaphoreType.DMA((len(OPPOSITE),)),
            pltpu.SemaphoreType.DMA((COPIES,)),
            pltpu.SemaphoreType.DMA((7,)),
        ],
        compiler_params=pltpu.CompilerParams(collective_id=0, has_side_effects=True),
        name="ptycho",
    )(
        positions.reshape(2), transmission.reshape(4, CORE, CORE), tv_weight, probe, fresnel_phase,
        amplitudes.reshape(PROBE, PROBE), jnp.asarray(tab),
    )
    return out.reshape(2, 2, CORE, CORE)


def solution(mesh):
    placed = (
        P(None, None, "row", "col"),
        P(),
        P(),
        P("row", "col", None, None, None),
        P("row", "col", None, None),
        P("row", "col"),
    )
    return jax.shard_map(
        body, mesh=mesh, in_specs=placed, out_specs=P(None, None, "row", "col"), check_vma=False
    )
```

```python
import functools
import math

import jax
import jax.numpy as jnp
import numpy as np
from jax import lax
from jax.experimental import pallas as pl
from jax.experimental.pallas import tpu as pltpu
from jax.sharding import PartitionSpec as P

MESH = pl.DeviceIdType.MESH
F32, BF16 = jnp.float32, jnp.bfloat16
CORE = 128
PROBE = 256
HALF = 128
HALO = 100
NEAR = PROBE - CORE - HALO
STRIP = 104
REACH = 3
EDGE = 8
TVROWS = CORE + EDGE
FOLD = 16
AMP_EPS = 0.1
LEARN_RATE = 0.2
TV_EPS = 1.0
TV_TAU = 0.1
TV_STEPS = 3


def tables():
    k, j = np.arange(HALF)[:, None], np.arange(HALF)[None, :]
    parts = []
    for odd in (0, 1):
        angle = 2.0 * np.pi * (((2 * k + odd) * j) % PROBE) / PROBE
        c, s = np.cos(angle) / math.sqrt(PROBE), np.sin(angle) / math.sqrt(PROBE)
        full = np.block([[c, s], [-s, c]])
        parts.append(full)
    out = []
    for full in (parts[0], parts[0].T, parts[1], parts[1].T):
        full = full.astype(np.float32)
        high = full.astype(BF16)
        out += [high, (full - high.astype(np.float32)).astype(BF16)]
    order = np.zeros((PROBE, PROBE), np.float32)
    order[np.arange(HALF), 2 * np.arange(HALF)] = 1
    order[HALF + np.arange(HALF), 2 * np.arange(HALF) + 1] = 1
    out += [order.astype(BF16), order.T.astype(BF16)]
    return np.stack(out)


def split(x):
    high = x.astype(BF16)
    return high, (x - high.astype(F32)).astype(BF16)


def mm(a, b):
    return jnp.dot(a, b, preferred_element_type=F32)


def left(tab, i, x):
    wh, wl = tab[2 * i], tab[2 * i + 1]
    xh, xl = split(x)
    return mm(wh, xh) + (mm(wh, xl) + mm(wl, xh))


def right(tab, i, x):
    wh, wl = tab[2 * i], tab[2 * i + 1]
    xh, xl = split(x)
    return mm(xh, wh) + (mm(xl, wh) + mm(xh, wl))


def cat(a, b, axis):
    return jnp.concatenate([a, b], axis=axis)


def forward(tab, re, im):
    h = HALF
    e = left(tab, 0, cat(re[:h] + re[h:], im[:h] + im[h:], 0))
    o = left(tab, 2, cat(re[:h] - re[h:], im[:h] - im[h:], 0))
    re, im = cat(e[:h], o[:h], 0), cat(e[h:], o[h:], 0)
    e = right(tab, 1, cat(re[:, :h] + re[:, h:], im[:, :h] + im[:, h:], 1))
    o = right(tab, 3, cat(re[:, :h] - re[:, h:], im[:, :h] - im[:, h:], 1))
    return cat(e[:, :h], o[:, :h], 1), cat(e[:, h:], o[:, h:], 1)


def inverse(tab, re, im):
    h = HALF
    e = left(tab, 1, cat(re[:h], im[:h], 0))
    o = left(tab, 3, cat(re[h:], im[h:], 0))
    s, d = e + o, e - o
    re, im = cat(s[:h], d[:h], 0), cat(s[h:], d[h:], 0)
    e = right(tab, 0, cat(re[:, :h], im[:, :h], 1))
    o = right(tab, 2, cat(re[:, h:], im[:, h:], 1))
    s, d = e + o, e - o
    return cat(s[:, :h], d[:, :h], 1), cat(s[:, h:], d[:, h:], 1)


def reorder(tab, x):
    for axis in (0, 1):
        total = None
        rest = x
        for _ in range(3):
            part = rest.astype(BF16)
            rest = rest - part.astype(F32)
            term = mm(tab[8], part) if axis == 0 else mm(part, tab[9])
            total = term if total is None else total + term
        x = total
    return x


class Place:
    def __init__(self):
        self.r, self.c = lax.axis_index("row"), lax.axis_index("col")
        self.nr, self.nc = lax.axis_size("row"), lax.axis_size("col")
        self.odd = lax.rem(self.r, 2)
        step = 1 - 2 * self.odd
        rows = {"mate": self.r + step, "other": self.r - step, "ahead": self.r + 2 * step, "behind": self.r - 2 * step}
        self.to = {side: {"row": at} for side, at in rows.items()}
        self.has = {side: (at >= 0) & (at < self.nr) for side, at in rows.items()}
        for side, at in (("left", self.c - 1), ("right", self.c + 1)):
            self.to[side] = {"col": at}
            self.has[side] = (at >= 0) & (at < self.nc)

    def signal(self):
        sem = pltpu.get_barrier_semaphore()
        for side in OPPOSITE:
            @pl.when(self.has[side])
            def _():
                pl.semaphore_signal(sem, inc=1, device_id=self.to[side], device_id_type=MESH)

    def wait(self):
        sem = pltpu.get_barrier_semaphore()
        pl.semaphore_wait(sem, sum(self.has[side].astype(jnp.int32) for side in OPPOSITE))


OPPOSITE = {"left": "right", "right": "left", "mate": "mate", "other": "other", "ahead": "behind", "behind": "ahead"}


class Wire:
    def __init__(self, place, send, recv):
        self.place, self.send, self.recv = place, send, recv
        self.count, self.all = 0, []

    def __call__(self, side, src, dst, sends=True, gets=True):
        copy = Copy(self.place, side, src, dst, self.send.at[list(OPPOSITE).index(side)], self.recv.at[self.count])
        copy.sends, copy.gets = copy.sends & sends, copy.gets & gets
        self.count += 1
        self.all.append(copy)
        return copy


class Copy:
    def __init__(self, place, side, src, dst, send, recv):
        self.op = pltpu.make_async_remote_copy(
            src_ref=src, dst_ref=dst, send_sem=send, recv_sem=recv, device_id=place.to[side], device_id_type=MESH,
        )
        self.sends, self.gets = place.has[side], place.has[OPPOSITE[side]]

    def start(self):
        pl.when(self.sends)(lambda: self.op.start())

    def got(self):
        pl.when(self.gets)(lambda: self.op.wait_recv())

    def sent(self):
        pl.when(self.sends)(lambda: self.op.wait_send())


def iota(shape, axis):
    return lax.broadcasted_iota(jnp.int32, shape, axis)


def tall(tile):
    return cat_rows([tile] * (CORE // EDGE))


def cat_rows(parts):
    return jnp.concatenate(parts, axis=0)


def compact(x):
    parts = [x[FOLD * k : FOLD * k + FOLD] for k in range(CORE // FOLD)]
    return parts[0] + sum(pltpu.roll(part, FOLD * k, 1) for k, part in enumerate(parts) if k)


def expand(x):
    return cat_rows([x] + [pltpu.roll(x, CORE - FOLD * k, 1) for k in range(1, CORE // FOLD)])


def squeeze(x, n):
    lane = iota(x.shape, 1)
    x = jnp.where((lane < REACH) | (lane >= CORE - REACH), x, 0.0)
    return pltpu.roll(x, REACH + 8 * n, 1)


def whole_kernel(
    pos_any, tr_any, w_any, probe_any, phase_any, amp_any, tab_any, out,
    pos, tile, w, probe, phase_ref, amp, tab,
    hl, hr, cl, cr, mt, nm, bridge, outl, outr, place_me, place_l, place_r, xs,
    w_rows, w_mate, w_other, w_pack, w_left, w_right,
    g, gl, gr, il, ir, tot, edge, side_out, side_in, near_out, near_in, mate_out, mate_in,
    fields, ptot, pedge, pbridge, pside_out, pside_in, pnear_out, pnear_in,
    send, recv, local,
):
    place = Place()
    has, odd = place.has, place.odd
    place.signal()
    loads = []
    pairs = (
        (tr_any, tile), (pos_any, pos), (phase_any, phase_ref), (tab_any, tab), (amp_any, amp), (probe_any, probe), (w_any, w),
    )
    for n, (src, dst) in enumerate(pairs):
        load = pltpu.make_async_copy(src, dst, local.at[n])
        load.start()
        loads.append(load)
    wire = Wire(place, send, recv)
    for side, refs in (
        ("left", (hl, cl, il, place_l, w_left)), ("right", (hr, cr, ir, place_r, w_right)),
        ("other", (nm, w_other, pside_in, *(side_in.at[ch] for ch in DIRECT_B), *(mate_in.at[ch] for ch in range(4) if ch not in DIRECT_B))),
        ("ahead", tuple(side_in.at[ch] for ch in range(4) if ch not in DIRECT_B)),
    ):
        @pl.when(jnp.logical_not(has[side]))
        def _():
            for ref in refs:
                ref[...] = jnp.zeros(ref.shape, F32)

    @pl.when(has["other"])
    def _():
        for ch in range(4):
            if ch not in DIRECT_B:
                near_in[ch] = jnp.zeros((CORE, CORE), F32)

    loads[1].wait()
    p, q = pos[0], pos[1]
    place_me[...] = jnp.full((EDGE, CORE), p.astype(F32))
    loads[0].wait()
    place.wait()

    low_strip = pl.ds(pl.multiple_of((CORE - STRIP) * odd, EDGE), STRIP)
    high_strip = pl.ds(pl.multiple_of((CORE - STRIP) * (1 - odd), EDGE), STRIP)
    half_strips = [
        pl.ds(pl.multiple_of((CORE - STRIP) * (1 - odd) + at, EDGE), size) for at, size in ((0, CUT), (CUT, STRIP - CUT))
    ]
    direct = {ch: wire("other", tile.at[ch, low_strip], nm.at[ch, low_strip]) for ch in DIRECT_A}
    to_mate = [
        wire("mate", *(ref.at[ch, high_strip if ch in (*direct, *VIA) else pl.ds(0, CORE)] for ref in (tile, mt))) for ch in range(4)
    ]
    slices = [pl.ds(2 * s, 2) for s in range(2)]
    to_left = [wire("left", tile.at[part], hr.at[part]) for part in slices]
    to_right = [wire("right", tile.at[part], hl.at[part]) for part in slices]
    via = {ch: wire("behind", tile.at[ch, low_strip], bridge.at[ch, low_strip]) for ch in VIA}
    across_via = {
        ch: wire("mate", bridge.at[ch, low_strip], nm.at[ch, low_strip], has["ahead"], has["other"]) for ch in VIA
    }
    relay = {
        ch: wire("ahead", mt.at[ch, high_strip], nm.at[ch, high_strip]) for ch in range(4) if ch not in (*direct, *via)
    }
    spots = [wire("left", place_me, place_r), wire("right", place_me, place_l)]
    corner_left = [wire("left", outl.at[ch], cr.at[ch]) for ch in range(4)]
    corner_right = [wire("right", outr.at[ch], cl.at[ch]) for ch in range(4)]
    w_steps = [wire("mate", w_rows, w_mate), wire("other", w_rows, w_other)]
    w_sides = [wire("left", w_pack, w_right), wire("right", w_pack, w_left)]
    for c in spots:
        c.start()
    for ch in VIA:
        via[ch].start()
    for ch in ORDER:
        if ch in direct:
            direct[ch].start()
        to_mate[ch].start()
        if ch % 2 == 0:
            to_left[ch // 2].start()
            to_right[ch // 2].start()
    loads[6].wait()
    w_rows[0:EDGE] = w[0:EDGE]
    w_rows[EDGE:] = w[CORE - EDGE :]
    for c in w_steps:
        c.start()

    sign = (1 - 2 * odd).astype(F32)
    block = (CORE, CORE)
    row = iota(block, 0).astype(F32) - (NEAR - 0.5)
    lane = iota(block, 1)
    sub = iota((EDGE, CORE), 0)
    nearer = lane < NEAR + q
    own_rows = row < p.astype(F32)

    def is_even(shape):
        return jnp.full(shape, odd, jnp.int32) == 0

    def forward_rows(channels):
        for ch in channels:
            to_mate[ch].got()
            if ch in relay:
                relay[ch].start()

    def forward_via(channels):
        for ch in channels:
            via[ch].got()
            across_via[ch].start()

    def forward_corners(channels):
        if 0 in channels:
            for c in spots:
                c.got()
        to_l = sign * (row - tall(place_l[...])) < 0
        to_r = sign * (row - tall(place_r[...])) < 0
        for ch in channels:
            {**direct, **across_via, **relay}[ch].got()
            m, n = mt[ch], nm[ch]
            outl[ch] = jnp.where(to_l, m, n)
            corner_left[ch].start()
            outr[ch] = jnp.where(to_r, m, n)
            corner_right[ch].start()

    mate_rows = sign * (row - p.astype(F32)) < 0

    def assemble(ch):
        if ch % 2 == 0:
            to_left[ch // 2].got()
            to_right[ch // 2].got()
        h = jnp.where(nearer, hr[ch], hl[ch])
        v = jnp.where(mate_rows, mt[ch], nm[ch])
        corner_left[ch].got()
        corner_right[ch].got()
        c = jnp.where(nearer, cr[ch], cl[ch])
        xs[ch] = cat(cat(tile[ch], h, 1), cat(v, c, 1), 0)

    loads[2].wait()
    loads[3].wait()
    phase = reorder(tab, phase_ref[...])
    kr, ki = jnp.cos(phase), jnp.sin(phase)
    loads[5].wait()
    turn_rows, turn_cols = p + (PROBE - HALO), q + (PROBE - HALO)
    pr, pi = (pltpu.roll(pltpu.roll(probe[n], turn_rows, 0), turn_cols, 1) for n in range(2))
    forward_via(VIA)
    forward_rows((0,))
    forward_corners((0,))
    loads[4].wait()
    measured = reorder(tab, amp[...])
    for ch in (1, 2, 3):
        forward_rows((ch,))
        forward_corners((ch,))
    assemble(0)
    assemble(1)
    ar, ai = xs[0], xs[1]
    fr, fi = forward(tab, ar * pr - ai * pi, ar * pi + ai * pr)
    wr, wi = inverse(tab, kr * fr - ki * fi, kr * fi + ki * fr)
    assemble(2)
    assemble(3)
    br, bi = xs[2], xs[3]
    fr, fi = forward(tab, br * wr - bi * wi, br * wi + bi * wr)
    for c in w_steps:
        c.got()
    thin = is_even((EDGE, CORE))
    below = jnp.where(thin, w_mate[0:EDGE], w_other[0:EDGE])
    above = jnp.where(thin, w_other[EDGE:], w_mate[EDGE:])
    w_edge = jnp.where(sub < EDGE // 2, below, above)
    w_pack[0:FOLD] = compact(squeeze(w[...], 0))
    w_pack[FOLD:] = squeeze(w_edge, 0)
    for c in w_sides:
        c.start()
    factor = 1.0 - measured * lax.rsqrt(fr * fr + fi * fi + AMP_EPS)
    gr_, gi_ = inverse(tab, fr * factor, fi * factor)

    across = {}
    lanes = iota((PROBE, CORE), 1)
    near_lanes = lanes < NEAR + q
    body_rows, rim_rows = pl.ds(0, CORE - 2 * EDGE), pl.ds(CORE - 2 * EDGE, PROBE - CORE + 2 * EDGE)

    def put(ch, grad):
        g[ch] = grad
        own, halo = grad[:, :CORE], grad[:, CORE:]
        to_r = jnp.where(lanes >= CORE - REACH, own, jnp.where(near_lanes, halo, 0.0))
        to_l = jnp.where(lanes < REACH, own, jnp.where(near_lanes, 0.0, halo))
        for n, (ref, x) in enumerate(((gr, to_r), (gl, to_l))):
            ref[ch] = cat_rows([x[EDGE:], x[:EDGE]])
        across[ch] = cross(ch, rim_rows)

    def cross(which, rows):
        pair = wire("right", gr.at[which, rows], il.at[which, rows]), wire("left", gl.at[which, rows], ir.at[which, rows])
        for c in pair:
            c.start()
        return pair

    upward, onward, beside, bridged = {}, {}, {}, {}

    lo, hi = CORE - STRIP, STRIP - EDGE

    def shares(first, last, down, up):
        even, thin = is_even(block), is_even((EDGE, CORE))
        rim = jnp.where(sub < REACH, down[:EDGE], jnp.where(sub >= EDGE - REACH, up[CORE - EDGE :], 0.0))
        up_far = cat_rows([up[:lo], jnp.where(sub < REACH, first, up[lo : lo + EDGE]), up[lo + EDGE :]])
        down_far = cat_rows([down[:hi], jnp.where(sub >= EDGE - REACH, last, down[hi : hi + EDGE]), down[hi + EDGE :]])
        far, near = jnp.where(even, up_far, down_far), jnp.where(even, down_far, up_far)
        mate_rim = jnp.where(thin, jnp.where(sub >= EDGE - REACH, last, 0.0), jnp.where(sub < REACH, first, 0.0))
        return rim, far, near, jnp.where(even, down, up), mate_rim

    bands = ((slice(0, EDGE), slice(PROBE - EDGE, PROBE)), (slice(CORE - EDGE, CORE), slice(CORE - 2 * EDGE, CORE - EDGE)))

    def joined(ch, mine, theirs):
        own, halo = g[ch, mine, :CORE], g[ch, mine, CORE:]
        fl, fr = il[ch, theirs], ir[ch, theirs]
        lane = iota(own.shape, 1)
        total = own + jnp.where(lane < CORE - REACH, fl, 0.0) + jnp.where(lane >= REACH, fr, 0.0)
        return total, halo + jnp.where(lane < REACH, fr, fl)

    packs = {}

    def fold(ch):
        s, n = divmod(ch, 2)
        for c in across[ch]:
            c.got()
        in_l = row < tall(place_l[...])
        in_r = row < tall(place_r[...])
        low = lane < REACH
        in_side = jnp.where(low, row - tall(place_r[...]), row - tall(place_l[...])) < 0
        far_rows = slice(CORE - EDGE, PROBE - EDGE)
        own, halo, fl, fr = g[ch, CORE:, :CORE], g[ch, CORE:, CORE:], il[ch, far_rows], ir[ch, far_rows]
        parts = ((own_rows, own), (in_l, jnp.where(lane < CORE - REACH, fl, 0.0)), (in_r, jnp.where(lane >= REACH, fr, 0.0)))
        down = sum(jnp.where(m, x, 0.0) for m, x in parts)
        up = sum(jnp.where(m, 0.0, x) for m, x in parts)
        ends = [joined(ch, *band) for band in bands]
        rim, far, near, base, mate_rim = shares(ends[0][0], ends[1][0], down, up)
        edge[ch], side_out[ch], near_out[ch] = rim, far, near
        strip = side_out.at[ch, high_strip], side_in.at[ch, high_strip]
        halves = [(side_out.at[ch, rows], side_in.at[ch, rows]) for rows in half_strips]
        near_strip = near_out.at[ch, low_strip], near_in.at[ch, low_strip]
        if ch in DIRECT_B:
            upward[ch] = wire("other", *strip)
            beside[ch] = wire("mate", *near_strip)
        else:
            upward[ch] = [wire("behind", *half) for half in halves]
            beside[ch] = wire("mate", *near_strip, jnp.logical_not(has["ahead"]), jnp.logical_not(has["other"]))
            mate_out[ch, :CORE], mate_out[ch, CORE:] = base, mate_rim
        for c in [upward[ch]] if ch in DIRECT_B else upward[ch]:
            c.start()
        beside[ch].start()
        o = jnp.where(low, fr, fl)
        pieces = [
            ends[0][1], ends[1][1],
            jnp.where(own_rows, halo, 0.0) + jnp.where(in_side, o, 0.0),
            jnp.where(own_rows, 0.0, halo) + jnp.where(in_side, 0.0, o),
        ]
        pieces = [squeeze(x, n) for x in pieces]
        if n == 0:
            packs[s] = pieces
            return
        pedge[s], far, near, _, _ = shares(*[a + b for a, b in zip(packs[s], pieces)])
        pside_out[s], pnear_out[s] = compact(far), compact(near)
        bridged[s] = wire("behind", pside_out.at[s], pbridge.at[s])
        upward[4 + s] = wire("mate", pbridge.at[s], pside_in.at[s], has["ahead"], has["other"])
        beside[4 + s] = wire("mate", pnear_out.at[s], pnear_in.at[s])
        bridged[s].start()
        beside[4 + s].start()

    def pass_pack(s):
        bridged[s].got()
        upward[4 + s].start()

    def fill(s):
        for c in inner[s]:
            c.got()
        for n in range(2):
            ch = 2 * s + n
            parts = [joined(ch, *bands[0])]
            parts.append(joined(ch, slice(EDGE, CORE - EDGE), slice(0, CORE - 2 * EDGE)))
            parts.append(joined(ch, *bands[1]))
            tot[ch] = cat_rows([x for x, _ in parts])
            margin = squeeze(cat_rows([x for _, x in parts]), n)
            ptot[s] = margin if n == 0 else ptot[s] + margin

    def incoming(x, turned=False):
        even, thin = is_even(block), is_even((EDGE, CORE))
        from_up, from_low = jnp.where(row < HALO - NEAR, x, 0.0), jnp.where(row > 0, x, 0.0)
        rim_low, rim_up = jnp.where(sub < REACH, x[lo : lo + EDGE], 0.0), jnp.where(sub >= EDGE - REACH, x[hi : hi + EDGE], 0.0)
        if turned:
            return jnp.where(even, from_up, from_low), jnp.where(thin, rim_up, rim_low)
        return jnp.where(even, from_low, from_up), jnp.where(thin, rim_low, rim_up)

    def pass_on(ch):
        onward[ch] = []
        for n, rows in enumerate((pl.ds(0, CUT), pl.ds(CUT, TVROWS - CUT))):
            upward[ch][n].got()
            if n == 0:
                x = side_in[ch, :CUT]
                mate_out[ch, :CUT] += jnp.where(is_even(x.shape), jnp.where(row[:CUT] > 0, x, 0.0), x)
            else:
                more, rim = incoming(side_in[ch])
                mate_out[ch, CUT:CORE] += more[CUT:]
                mate_out[ch, CORE:] += rim
            onward[ch].append(wire("mate", mate_out.at[ch, rows], mate_in.at[ch, rows], has["ahead"], has["other"]))
            onward[ch][n].start()

    def total(ch):
        beside[ch].got()
        a, ra = incoming(near_in[ch])
        if ch in DIRECT_B:
            upward[ch].got()
            b, rb = incoming(side_in[ch], True)
        else:
            for c in onward[ch]:
                c.got()
            b, rb = mate_in[ch, :CORE], mate_in[ch, CORE:]
        return cat_rows([a + b, ra + rb])

    shape = (TVROWS, PROBE)

    def prepare(s):
        rest = cat_rows([ptot[s], pedge[s]])
        for n in range(2):
            ch = 2 * s + n
            grad = cat(cat_rows([tot[ch], edge[ch]]), pltpu.roll(rest, CORE - REACH - 8 * n, 1), 1)
            wide = iota((EDGE, PROBE), 0) < EDGE // 2
            rim = jnp.where(wide, xs[ch, CORE : CORE + EDGE, :], xs[ch, PROBE - EDGE :, :])
            fields[ch] = (cat_rows([xs[ch, :CORE, :], rim]) - LEARN_RATE * grad) * inside

    def smooth(s):
        upward[4 + s].got()
        beside[4 + s].got()
        (a, ra), (b, rb) = incoming(expand(pnear_in[s])), incoming(expand(pside_in[s]), True)
        rest = cat_rows([a + b, ra + rb])
        pair = []
        for n in range(2):
            ch = 2 * s + n
            grad = cat(total(ch), pltpu.roll(rest, CORE - REACH - 8 * n, 1), 1)
            pair.append(fields[ch] - LEARN_RATE * inside * grad)
        march(s, pair)

    def march(s, pair):
        count = CORE // EDGE + 2
        at = iota((EDGE, PROBE), 0)

        def tiles(x):
            rows = [x[EDGE * k : EDGE * k + EDGE] for k in range(TVROWS // EDGE)]
            return rows[-1:] + rows

        kept, weights = tiles(inside), tiles(TV_TAU * weight)
        done = {(0, n, k): t for n in range(2) for k, t in enumerate(tiles(pair[0]) if n == 0 else tiles(pair[1]))}
        memo = {}

        def once(key, make):
            if key not in memo:
                memo[key] = make()
            return memo[key]

        def field(step, n, k):
            if (step, n, k) not in done:
                f = field(step - 1, n, k)
                d, r = flux(step - 1, k)[n]
                before = fallen(step - 1, n, k - 1) if k else fallen(step - 1, n, k)
                d = d - jnp.where(at == 0, before, fallen(step - 1, n, k))
                done[step, n, k] = (f + (d + (r - pltpu.roll(r, 1, 1)))) * kept[k]
            return done[step, n, k]

        def raised(step, n, k):
            return once(("up", step, n, k), lambda: pltpu.roll(field(step, n, k), EDGE - 1, 0))

        def fallen(step, n, k):
            return once(("down", step, n, k), lambda: pltpu.roll(flux(step, k)[n][0], 1, 0))

        def flux(step, k):
            def make():
                down, right = [], []
                for n in range(2):
                    f = field(step, n, k)
                    below = raised(step, n, min(k + 1, count - 1))
                    down.append(jnp.where(at == EDGE - 1, below, raised(step, n, k)) - f)
                    right.append(pltpu.roll(f, PROBE - 1, 1) - f)
                square = down[0] * down[0] + right[0] * right[0] + (down[1] * down[1] + right[1] * right[1])
                gain = weights[k] * lax.rsqrt(square + TV_EPS)
                return [(gain * d, gain * r) for d, r in zip(down, right)]
            return once(("flux", step, k), make)

        for k in range(1, count - 1):
            for n in range(2):
                out[2 * s + n, EDGE * (k - 1) : EDGE * k] = field(TV_STEPS, n, k)[:, :CORE]

    put(2, wr * gr_ + wi * gi_)
    put(3, wr * gi_ - wi * gr_)
    fr, fi = forward(tab, br * gr_ + bi * gi_, br * gi_ - bi * gr_)
    gr_, gi_ = inverse(tab, kr * fr + ki * fi, kr * fi - ki * fr)
    put(0, pr * gr_ + pi * gi_)
    put(1, pr * gi_ - pi * gr_)
    inner = {s: cross(pl.ds(2 * s, 2), body_rows) for s in (1, 0)}
    fold(2)
    fold(3)
    for c in w_sides:
        c.got()
    row_at, col_at = iota(shape, 0), iota(shape, 1)
    row_at = place.r * CORE + jnp.where(row_at < CORE + EDGE // 2, row_at, row_at - TVROWS)
    col_at = place.c * CORE + jnp.where(col_at < CORE + HALF // 2, col_at, col_at - PROBE)
    inside = (row_at >= 0) & (row_at < place.nr * CORE) & (col_at >= 0) & (col_at < place.nc * CORE)
    inside = inside.astype(F32)
    margins = [cat_rows([expand(ref[:FOLD]), ref[FOLD:]]) for ref in (w_right, w_left)]
    margins = [pltpu.roll(m, CORE - REACH, 1) for m in margins]
    far = jnp.where(iota((TVROWS, CORE), 1) < HALF // 2, margins[0], margins[1])
    weight = cat(cat_rows([w[...], w_edge]), far, 1) * inside
    fold(0)
    fold(1)
    pass_on(2)
    pass_pack(1)
    pass_on(0)
    pass_pack(0)
    fill(1)
    prepare(1)
    fill(0)
    prepare(0)
    smooth(1)
    smooth(0)
    assert wire.count == COPIES
    for c in wire.all:
        c.sent()


COPIES = 60
CUT = 56
ORDER = (0, 1, 2, 3)
DIRECT_A = (0, 1)
VIA = (2, 3)
DIRECT_B = (1, 3)


def body(transmission, probe, fresnel_phase, amplitudes, positions, tv_weight):
    vmem, anywhere = (pl.BlockSpec(memory_space=m) for m in (pltpu.VMEM, pl.ANY))
    tab = tables()

    def scratch(*shape):
        return pltpu.VMEM(shape, F32)

    four = lambda n: [scratch(4, CORE, CORE)] * n
    small = lambda n: [scratch(EDGE, CORE)] * n
    out = pl.pallas_call(
        whole_kernel,
        out_shape=pltpu.VMEM((4, CORE, CORE), F32),
        in_specs=[anywhere] * 7,
        out_specs=vmem,
        scratch_shapes=[
            pltpu.SMEM((2,), jnp.int32), scratch(4, CORE, CORE), scratch(CORE, CORE), scratch(2, PROBE, PROBE),
            scratch(PROBE, PROBE), scratch(PROBE, PROBE), pltpu.VMEM(tab.shape, BF16),
            *four(9), *small(3), scratch(4, PROBE, PROBE),
            *[scratch(2 * EDGE, CORE)] * 3, *[scratch(FOLD + EDGE, CORE)] * 3,
            scratch(4, PROBE, PROBE), *[scratch(4, PROBE, CORE)] * 4,
            scratch(4, CORE, CORE), scratch(4, EDGE, CORE), *four(4), *[scratch(4, TVROWS, CORE)] * 2,
            scratch(4, TVROWS, PROBE), scratch(2, CORE, CORE), scratch(2, EDGE, CORE), *[scratch(2, FOLD, CORE)] * 5,
            pltpu.SemaphoreType.DMA((len(OPPOSITE),)),
            pltpu.SemaphoreType.DMA((COPIES,)),
            pltpu.SemaphoreType.DMA((7,)),
        ],
        compiler_params=pltpu.CompilerParams(collective_id=0, has_side_effects=True),
        name="ptycho",
    )(
        positions.reshape(2), transmission.reshape(4, CORE, CORE), tv_weight, probe, fresnel_phase,
        amplitudes.reshape(PROBE, PROBE), jnp.asarray(tab),
    )
    return out.reshape(2, 2, CORE, CORE)


def solution(mesh):
    placed = (
        P(None, None, "row", "col"),
        P(),
        P(),
        P("row", "col", None, None, None),
        P("row", "col", None, None),
        P("row", "col"),
    )
    return jax.shard_map(
        body, mesh=mesh, in_specs=placed, out_specs=P(None, None, "row", "col"), check_vma=False
    )
```
